32 devices in a mesh: group: 2 (over y), dev: 16 (over z, x, core).
Axes of the slice: x: 2, y: 2, z: 4, core: 2. Of those that a mesh axis runs over, the one named last changes fastest.
Arguments:
- mantissa: bfloat16 [64, 32, 896], P(None, ('group', 'dev')), may hold values from 0.5 to 1
- exponent: int32 [64, 32, 7], P(None, ('group', 'dev')), may hold values from 1 to 4
- poly_square: float32 [896], replicated, may hold values from 0.02 to 0.2
- poly_cube: float32 [896], replicated, may hold values from 0.005 to 0.05
- col_map: bfloat16 [896, 896], replicated, may hold values from -0.1875 to 0.1875
- rebin_offset: int32 [32, 7], P('group'), may hold values from -8 to 7
- rebin_weight: float32 [32, 7], P('group'), may hold values from 0 to 1
- kern_first: bfloat16 [32, 3, 3], replicated, may hold values from -2 to 2
- kern_second: bfloat16 [32, 32, 3, 3], replicated, may hold values from -0.375 to 0.375
- kern_last: bfloat16 [32], replicated, may hold values from -1 to 1
Outputs:
- dual: bfloat16 [64, 32, 896], P('dev', 'group')
The draws below stay inside these ranges and needn't reach their ends.
Inputs may be any that keep to these rules, and one draw needn't show every extreme that they name: `rebin_offset`: interpolation sources of rebinned view v lie in views v - 8 to v + 8.
All inputs are finite; a program needn't handle non-finite values.
Results may differ from the reference program's by a relative error of at most 0.0065.
Values may be sent and summed in bfloat16 or wider, within the bound.
No kernel may reach another device: no remote copies, remote signals or barrier semaphores. Data moves between devices by JAX's collectives and lax.ppermute only.
A program may use at most 64 MiB of HBM per device.

```python
import math
import jax
import jax.numpy as jnp
from jax import lax

DR = 64
DC = 896
COLB = 128
CH = 32
REACH = 8
VIEWS = 32


def plant(values, key, least, high):
    dims = values.shape
    spot = [jax.random.randint(jax.random.fold_in(key, axis), (), 0, dims[axis]) for axis in range(len(dims))]
    values = values.at[tuple(spot)].set(least)
    longest = dims.index(max(dims))
    spot[longest] = (spot[longest] + 1) % dims[longest]
    return values.at[tuple(spot)].set(high)


def block_levels(stream_key, extent, split, smallest, high):
    def one(dim, parts):
        heights = jax.random.uniform(jax.random.fold_in(jax.random.fold_in(stream_key, 6), dim), (parts,), jnp.float32, smallest / len(split), high / len(split))
        return jnp.repeat(jnp.exp(heights), extent[dim] // parts).reshape((-1,) + (1,) * (len(extent) - dim - 1))

    factor_of = one(*split[0])
    for cut in split[1:]:
        factor_of = factor_of * one(*cut)
    return factor_of


def bell_draw(stream_key, extent, scale, most, kind=jnp.bfloat16):
    return jnp.clip(scale * jax.random.normal(stream_key, extent, jnp.float32), -most, most).astype(kind)


def setup_inputs(seed: int = 0) -> dict:
    splits = jax.random.split(jax.random.key(seed), 11)
    return {
        "mantissa": jnp.clip(0.5 + 0.5 * jax.random.uniform(splits[0], (DR, VIEWS, DC), jnp.float32) ** block_levels(splits[0], (DR, VIEWS, DC), ((1, 32),), -0.2, 0.2), 0.5, 1.0).astype(jnp.bfloat16),
        "exponent": plant(jax.random.randint(splits[1], (DR, VIEWS, DC // COLB), 1, 5), jax.random.fold_in(splits[1], 1), 1, 4).astype(jnp.int32),
        "poly_square": jnp.clip(jnp.exp(jax.random.uniform(splits[2], (DC,), jnp.float32, math.log(0.02), math.log(0.2))), 0.02, 0.2),
        "poly_cube": jnp.clip(jnp.exp(jax.random.uniform(splits[3], (DC,), jnp.float32, math.log(0.005), math.log(0.05))), 0.005, 0.05),
        "col_map": bell_draw(splits[4], (DC, DC), DC ** -0.5, 0.1875),
        "rebin_offset": plant(jax.random.randint(splits[5], (VIEWS, DC // COLB), -REACH, REACH), jax.random.fold_in(splits[5], 1), -REACH, REACH - 1).astype(jnp.int32),
        "rebin_weight": jnp.clip(1.0 * jax.random.uniform(splits[6], (VIEWS, DC // COLB), jnp.float32) ** block_levels(splits[6], (VIEWS, DC // COLB), ((0, 2),), -0.2, 0.2), 0.0, 1.0),
        "kern_first": bell_draw(splits[7], (CH, 3, 3), 9 ** -0.5, 2.0),
        "kern_second": bell_draw(splits[8], (CH, CH, 3, 3), (CH * 9) ** -0.5, 0.375),
        "kern_last": bell_draw(splits[9], (CH,), CH ** -0.5, 1.0),
    }


def reference(mantissa, exponent, poly_square, poly_cube, col_map, rebin_offset, rebin_weight, kern_first, kern_second, kern_last):
    block_count = DC // COLB
    counts = mantissa.astype(jnp.float32).reshape(DR, VIEWS, block_count, COLB)
    counts = counts * jnp.exp2(-exponent.astype(jnp.float32))[..., None]
    line_int = -jnp.log(counts).reshape(DR, VIEWS, DC)
    hardened = (line_int + poly_square * line_int * line_int + poly_cube * line_int * line_int * line_int).astype(jnp.bfloat16)
    projected = jnp.dot(hardened.reshape(DR * VIEWS, DC), col_map, preferred_element_type=jnp.float32)
    projected = projected.astype(jnp.bfloat16).reshape(DR, VIEWS, DC)
    lower_idx = jnp.arange(VIEWS, dtype=jnp.int32)[:, None] + rebin_offset.astype(jnp.int32) + REACH
    block_ids = jnp.arange(block_count, dtype=jnp.int32)[None, :]
    frac = rebin_weight[:, :, None]
    weights_first = kern_first.astype(jnp.float32).reshape(CH, 1, 3, 3)
    weights_second = kern_second.astype(jnp.float32)
    weights_last = kern_last.astype(jnp.float32)
    numbers = ("NCHW", "OIHW", "NCHW")

    def one_row(row_proj):
        extended = jnp.pad(row_proj, ((REACH, REACH), (0, 0))).reshape(VIEWS + 2 * REACH, block_count, COLB)
        lower = extended[lower_idx, block_ids].astype(jnp.float32)
        upper = extended[lower_idx + 1, block_ids].astype(jnp.float32)
        signal = ((1.0 - frac) * lower + frac * upper).astype(jnp.bfloat16).reshape(VIEWS, DC)
        image = signal.astype(jnp.float32)[None, None]
        first = lax.conv_general_dilated(image, weights_first, (1, 1), ((1, 1), (1, 1)), dimension_numbers=numbers, precision=lax.Precision.HIGHEST)
        first = lax.optimization_barrier(jnp.maximum(first, 0.0).astype(jnp.bfloat16)).astype(jnp.float32)
        second = lax.conv_general_dilated(first, weights_second, (1, 1), ((1, 1), (1, 1)), dimension_numbers=numbers, precision=lax.Precision.HIGHEST)
        second = lax.optimization_barrier(jnp.maximum(second, 0.0).astype(jnp.bfloat16)).astype(jnp.float32)
        mixed = signal.astype(jnp.float32) + jnp.einsum("i,ivc->vc", weights_last, second[0], precision=lax.Precision.HIGHEST)
        return mixed.astype(jnp.bfloat16)

    return lax.map(one_row, projected)
```

```python
import jax
import jax.numpy as jnp
from jax import lax
from jax.sharding import PartitionSpec as P

REACH = 8
RIM = 2


def halo_exchange(block, axis, dim, width):
    count = lax.axis_size(axis)
    forward = [(i, i + 1) for i in range(count - 1)]
    backward = [(target, source) for source, target in forward]
    low = lax.ppermute(
        lax.slice_in_dim(block, block.shape[dim] - width, None, axis=dim), axis, forward
    )
    high = lax.ppermute(lax.slice_in_dim(block, 0, width, axis=dim), axis, backward)
    return low, high


def prepare(mantissa, exponent, poly_square, poly_cube):
    lead_rows, lead_views, width_all = mantissa.shape
    block_count = exponent.shape[2]
    counts = mantissa.astype(jnp.float32).reshape(
        lead_rows, lead_views, block_count, width_all // block_count
    )
    counts = counts * jnp.exp2(-exponent.astype(jnp.float32))[..., None]
    line_int = -jnp.log(counts).reshape(lead_rows, lead_views, width_all)
    hardened = (
        line_int + poly_square * line_int * line_int + poly_cube * line_int * line_int * line_int
    )
    return hardened.astype(jnp.bfloat16)


def resample(hardened, col_map):
    shape_in = hardened.shape
    flat = hardened.reshape(-1, shape_in[2])
    product = jnp.dot(flat, col_map, preferred_element_type=jnp.float32)
    return product.astype(jnp.bfloat16).reshape(shape_in)


def local(
    mantissa,
    exponent,
    poly_square,
    poly_cube,
    col_map,
    rebin_offset,
    rebin_weight,
    kern_first,
    kern_second,
    kern_last,
):
    width_all = mantissa.shape[2]
    block_count = exponent.shape[2]
    col_block = width_all // block_count
    projected = resample(prepare(mantissa, exponent, poly_square, poly_cube), col_map)
    row_major = lax.all_to_all(projected, "dev", split_axis=0, concat_axis=1, tiled=True)
    row_count, view_count = (row_major.shape[0], row_major.shape[1])
    group_idx = lax.axis_index("group")
    total_views = view_count * lax.axis_size("group")
    view_start = group_idx * view_count
    halo = REACH + RIM

    params = jnp.stack([rebin_offset.astype(jnp.float32), rebin_weight], axis=0)
    low, high = halo_exchange(row_major, "group", 1, halo)
    params_low, params_high = halo_exchange(params, "group", 1, RIM)
    extended = jnp.concatenate([low, row_major, high], axis=1)
    params_ext = jnp.concatenate([params_low, params, params_high], axis=1)

    sig_views = view_count + 2 * RIM
    offset_ext = params_ext[0].astype(jnp.int32)
    weight_ext = params_ext[1]
    extended = extended.reshape(row_count, view_count + 2 * halo, block_count, col_block)
    lower_idx = jnp.arange(sig_views, dtype=jnp.int32)[:, None] + offset_ext + REACH
    block_ids = jnp.arange(block_count, dtype=jnp.int32)[None, :]
    lower = extended[:, lower_idx, block_ids, :].astype(jnp.float32)
    upper = extended[:, lower_idx + 1, block_ids, :].astype(jnp.float32)
    frac = weight_ext[None, :, :, None]
    signal = ((1.0 - frac) * lower + frac * upper).reshape(row_count, sig_views, width_all)
    sig_pos = view_start - RIM + jnp.arange(sig_views, dtype=jnp.int32)
    sig_valid = (sig_pos >= 0) & (sig_pos < total_views)
    signal = jnp.where(sig_valid[None, :, None], signal, 0.0).astype(jnp.bfloat16)

    numbers = ("NCHW", "OIHW", "NCHW")
    first = lax.conv_general_dilated(
        signal[:, None],
        kern_first[:, None],
        (1, 1),
        ((0, 0), (1, 1)),
        dimension_numbers=numbers,
        preferred_element_type=jnp.float32,
    )
    first_pos = view_start - 1 + jnp.arange(view_count + 2, dtype=jnp.int32)
    first_valid = (first_pos >= 0) & (first_pos < total_views)
    first = jnp.where(first_valid[None, None, :, None], jnp.maximum(first, 0.0), 0.0)
    first = first.astype(jnp.bfloat16)
    second = lax.conv_general_dilated(
        first,
        kern_second,
        (1, 1),
        ((0, 0), (1, 1)),
        dimension_numbers=numbers,
        preferred_element_type=jnp.float32,
    )
    second = jnp.maximum(second, 0.0).astype(jnp.bfloat16)
    mixed = signal[:, RIM : RIM + view_count].astype(jnp.float32) + jnp.einsum(
        "i,rivc->rvc", kern_last, second, preferred_element_type=jnp.float32
    )
    return mixed.astype(jnp.bfloat16)


def solution(mesh):
    return jax.shard_map(
        local,
        mesh=mesh,
        in_specs=(
            P(None, ("group", "dev"), None),
            P(None, ("group", "dev"), None),
            P(),
            P(),
            P(),
            P("group", None),
            P("group", None),
            P(),
            P(),
            P(),
        ),
        out_specs=P("dev", "group", None),
        check_vma=False,
    )
```

```python
import functools

import jax
import jax.numpy as jnp
from jax import lax
from jax.experimental import pallas as pl
from jax.experimental.pallas import tpu as pltpu
from jax.sharding import PartitionSpec as P

REACH = 8
RIM = 2


def halo_exchange(block, axis, dim, width):
    count = lax.axis_size(axis)
    forward = [(i, i + 1) for i in range(count - 1)]
    backward = [(target, source) for source, target in forward]
    low = lax.ppermute(
        lax.slice_in_dim(block, block.shape[dim] - width, None, axis=dim), axis, forward
    )
    high = lax.ppermute(lax.slice_in_dim(block, 0, width, axis=dim), axis, backward)
    return low, high


def conv_kernel(bounds_ref, sig_ref, w1_ref, w2_ref, kl_ref, out_ref, feat_ref, dual_ref, *, first_views, out_views, width, channels):
    view_start = bounds_ref[0]
    total_views = bounds_ref[1]
    col = lax.broadcasted_iota(jnp.int32, (channels, width), 1)
    keep_left = col >= 1
    keep_right = col < width - 1
    w1 = w1_ref[...]
    for u in range(first_views):
        taps = sig_ref[0, 3 * u : 3 * u + 16, :].astype(jnp.bfloat16)
        hidden = jnp.dot(w1, taps, preferred_element_type=jnp.float32)
        pos = view_start - 1 + u
        scale = ((pos >= 0) & (pos < total_views)).astype(jnp.float32)
        hidden = jnp.maximum(hidden, 0.0) * scale
        base = 3 * u * channels
        feat_ref[base : base + channels, :] = jnp.where(keep_left, pltpu.roll(hidden, 1, 1), 0.0).astype(jnp.bfloat16)
        feat_ref[base + channels : base + 2 * channels, :] = hidden.astype(jnp.bfloat16)
        feat_ref[base + 2 * channels : base + 3 * channels, :] = jnp.where(
            keep_right, pltpu.roll(hidden, width - 1, 1), 0.0
        ).astype(jnp.bfloat16)
    w2 = w2_ref[...]
    kl = kl_ref[...]
    for v in range(out_views):
        window = feat_ref[3 * v * channels : 3 * (v + 3) * channels, :]
        second = jnp.dot(w2, window, preferred_element_type=jnp.float32)
        second = jnp.maximum(second, 0.0).astype(jnp.bfloat16).astype(jnp.float32)
        mix = jnp.sum(kl * second, axis=0, keepdims=True)
        centre = sig_ref[0, 3 * (v + 2) + 1 : 3 * (v + 2) + 2, :]
        dual_ref[v : v + 1, :] = centre + mix
    out_ref[0] = dual_ref[...].astype(out_ref.dtype)


def dual_conv(signal, bounds, kern_first, kern_second, kern_last):
    rows, sig_views, width = signal.shape
    channels = kern_first.shape[0]
    first_views = sig_views - 2
    out_views = sig_views - 4
    zero = jnp.zeros_like(signal[..., :1])
    left = jnp.concatenate([zero, signal[..., :-1]], axis=-1)
    right = jnp.concatenate([signal[..., 1:], zero], axis=-1)
    stacked = jnp.stack([left, signal, right], axis=2).astype(jnp.float32)
    stacked = stacked.reshape(rows, sig_views * 3, width)
    pad_rows = -(-(3 * first_views + 13) // 8) * 8
    stacked = jnp.pad(stacked, ((0, 0), (0, pad_rows - sig_views * 3), (0, 0)))
    w1 = jnp.pad(kern_first.reshape(channels, 9), ((0, 0), (0, 7)))
    w2 = jnp.transpose(kern_second, (0, 2, 3, 1)).reshape(channels, 9 * channels)
    kl = kern_last.astype(jnp.float32).reshape(channels, 1)
    kernel = functools.partial(conv_kernel, first_views=first_views, out_views=out_views, width=width, channels=channels)
    return pl.pallas_call(
        kernel,
        out_shape=jax.ShapeDtypeStruct((rows, out_views, width), jnp.bfloat16),
        grid=(rows,),
        in_specs=[
            pl.BlockSpec(memory_space=pltpu.SMEM),
            pl.BlockSpec((1, pad_rows, width), lambda r: (r, 0, 0)),
            pl.BlockSpec((channels, 16), lambda r: (0, 0)),
            pl.BlockSpec((channels, 9 * channels), lambda r: (0, 0)),
            pl.BlockSpec((channels, 1), lambda r: (0, 0)),
        ],
        out_specs=pl.BlockSpec((1, out_views, width), lambda r: (r, 0, 0)),
        scratch_shapes=[
            pltpu.VMEM((first_views * 3 * channels, width), jnp.bfloat16),
            pltpu.VMEM((out_views, width), jnp.float32),
        ],
    )(bounds, stacked, w1.astype(jnp.bfloat16), w2.astype(jnp.bfloat16), kl)


def prepare(mantissa, exponent, poly_square, poly_cube):
    lead_rows, lead_views, width_all = mantissa.shape
    block_count = exponent.shape[2]
    counts = mantissa.astype(jnp.float32).reshape(
        lead_rows, lead_views, block_count, width_all // block_count
    )
    counts = counts * jnp.exp2(-exponent.astype(jnp.float32))[..., None]
    line_int = -jnp.log(counts).reshape(lead_rows, lead_views, width_all)
    hardened = (
        line_int + poly_square * line_int * line_int + poly_cube * line_int * line_int * line_int
    )
    return hardened.astype(jnp.bfloat16)


def resample(hardened, col_map):
    shape_in = hardened.shape
    flat = hardened.reshape(-1, shape_in[2])
    product = jnp.dot(flat, col_map, preferred_element_type=jnp.float32)
    return product.astype(jnp.bfloat16).reshape(shape_in)


def local(
    mantissa,
    exponent,
    poly_square,
    poly_cube,
    col_map,
    rebin_offset,
    rebin_weight,
    kern_first,
    kern_second,
    kern_last,
):
    width_all = mantissa.shape[2]
    block_count = exponent.shape[2]
    col_block = width_all // block_count
    projected = resample(prepare(mantissa, exponent, poly_square, poly_cube), col_map)
    row_major = lax.all_to_all(projected, "dev", split_axis=0, concat_axis=1, tiled=True)
    row_count, view_count = (row_major.shape[0], row_major.shape[1])
    group_idx = lax.axis_index("group")
    total_views = view_count * lax.axis_size("group")
    view_start = group_idx * view_count
    halo = REACH + RIM

    params = jnp.stack([rebin_offset.astype(jnp.float32), rebin_weight], axis=0)
    low, high = halo_exchange(row_major, "group", 1, halo)
    params_low, params_high = halo_exchange(params, "group", 1, RIM)
    extended = jnp.concatenate([low, row_major, high], axis=1)
    params_ext = jnp.concatenate([params_low, params, params_high], axis=1)

    sig_views = view_count + 2 * RIM
    offset_ext = params_ext[0].astype(jnp.int32)
    weight_ext = params_ext[1]
    extended = extended.reshape(row_count, view_count + 2 * halo, block_count, col_block)
    lower_idx = jnp.arange(sig_views, dtype=jnp.int32)[:, None] + offset_ext + REACH
    block_ids = jnp.arange(block_count, dtype=jnp.int32)[None, :]
    lower = extended[:, lower_idx, block_ids, :].astype(jnp.float32)
    upper = extended[:, lower_idx + 1, block_ids, :].astype(jnp.float32)
    frac = weight_ext[None, :, :, None]
    signal = ((1.0 - frac) * lower + frac * upper).reshape(row_count, sig_views, width_all)
    sig_pos = view_start - RIM + jnp.arange(sig_views, dtype=jnp.int32)
    sig_valid = (sig_pos >= 0) & (sig_pos < total_views)
    signal = jnp.where(sig_valid[None, :, None], signal, 0.0).astype(jnp.bfloat16)

    bounds = jnp.stack([view_start, total_views]).astype(jnp.int32)
    return dual_conv(signal, bounds, kern_first, kern_second, kern_last)


def solution(mesh):
    return jax.shard_map(
        local,
        mesh=mesh,
        in_specs=(
            P(None, ("group", "dev"), None),
            P(None, ("group", "dev"), None),
            P(),
            P(),
            P(),
            P("group", None),
            P("group", None),
            P(),
            P(),
            P(),
        ),
        out_specs=P("dev", "group", None),
        check_vma=False,
    )
```

```python
import functools

import jax
import jax.numpy as jnp
from jax import lax
from jax.experimental import pallas as pl
from jax.experimental.pallas import tpu as pltpu
from jax.sharding import PartitionSpec as P

REACH = 8
RIM = 2


def halo_exchange(block, axis, dim, width):
    count = lax.axis_size(axis)
    forward = [(i, i + 1) for i in range(count - 1)]
    backward = [(target, source) for source, target in forward]
    low = lax.ppermute(
        lax.slice_in_dim(block, block.shape[dim] - width, None, axis=dim), axis, forward
    )
    high = lax.ppermute(lax.slice_in_dim(block, 0, width, axis=dim), axis, backward)
    return low, high


def conv_kernel(
    offset_ref,
    weight_ref,
    bounds_ref,
    ext_ref,
    w1_ref,
    w2_ref,
    kl_ref,
    out_ref,
    sig_ref,
    feat_ref,
    dual_ref,
    *,
    sig_views,
    block_count,
    col_block,
    channels,
):
    width = block_count * col_block
    first_views = sig_views - 2
    out_views = sig_views - 4
    view_start = bounds_ref[0]
    total_views = bounds_ref[1]
    lane = lax.broadcasted_iota(jnp.int32, (1, width), 1)
    sig_ref[3 * sig_views :, :] = jnp.zeros((sig_ref.shape[0] - 3 * sig_views, width), jnp.float32)
    for u in range(sig_views):
        pos = view_start - RIM + u
        keep = ((pos >= 0) & (pos < total_views)).astype(jnp.float32)
        for k in range(block_count):
            low = u + offset_ref[u * block_count + k] + REACH
            frac = weight_ref[u * block_count + k]
            cols = pl.ds(k * col_block, col_block)
            lower = ext_ref[0, low, :, cols]
            upper = ext_ref[0, low + 1, :, cols]
            value = ((1.0 - frac) * lower + frac * upper).astype(jnp.bfloat16)
            sig_ref[3 * u + 1 : 3 * u + 2, cols] = value.astype(jnp.float32) * keep
        row = sig_ref[3 * u + 1 : 3 * u + 2, :]
        sig_ref[3 * u : 3 * u + 1, :] = jnp.where(lane >= 1, pltpu.roll(row, 1, 1), 0.0)
        sig_ref[3 * u + 2 : 3 * u + 3, :] = jnp.where(
            lane < width - 1, pltpu.roll(row, width - 1, 1), 0.0
        )
    col = lax.broadcasted_iota(jnp.int32, (channels, width), 1)
    keep_left = col >= 1
    keep_right = col < width - 1
    w1 = w1_ref[...]
    for u in range(first_views):
        taps = sig_ref[3 * u : 3 * u + 16, :].astype(jnp.bfloat16)
        hidden = jnp.dot(w1, taps, preferred_element_type=jnp.float32)
        pos = view_start - 1 + u
        scale = ((pos >= 0) & (pos < total_views)).astype(jnp.float32)
        hidden = jnp.maximum(hidden, 0.0) * scale
        base = 3 * u * channels
        feat_ref[base : base + channels, :] = jnp.where(
            keep_left, pltpu.roll(hidden, 1, 1), 0.0
        ).astype(jnp.bfloat16)
        feat_ref[base + channels : base + 2 * channels, :] = hidden.astype(jnp.bfloat16)
        feat_ref[base + 2 * channels : base + 3 * channels, :] = jnp.where(
            keep_right, pltpu.roll(hidden, width - 1, 1), 0.0
        ).astype(jnp.bfloat16)
    w2 = w2_ref[...]
    kl = kl_ref[...]
    for v in range(out_views):
        window = feat_ref[3 * v * channels : 3 * (v + 3) * channels, :]
        second = jnp.dot(w2, window, preferred_element_type=jnp.float32)
        second = jnp.maximum(second, 0.0).astype(jnp.bfloat16).astype(jnp.float32)
        mix = jnp.sum(kl * second, axis=0, keepdims=True)
        centre = sig_ref[3 * (v + 2) + 1 : 3 * (v + 2) + 2, :]
        dual_ref[v : v + 1, :] = centre + mix
    out_ref[0] = dual_ref[...].astype(out_ref.dtype)


def rebin_dual(extended, offsets, weights, bounds, kern_first, kern_second, kern_last):
    rows, ext_views, width = extended.shape
    sig_views, block_count = offsets.shape
    col_block = width // block_count
    channels = kern_first.shape[0]
    first_views = sig_views - 2
    out_views = sig_views - 4
    pad_rows = -(-(3 * first_views + 13) // 8) * 8
    w1 = jnp.pad(kern_first.reshape(channels, 9), ((0, 0), (0, 7)))
    w2 = jnp.transpose(kern_second, (0, 2, 3, 1)).reshape(channels, 9 * channels)
    kl = kern_last.astype(jnp.float32).reshape(channels, 1)
    kernel = functools.partial(
        conv_kernel,
        sig_views=sig_views,
        block_count=block_count,
        col_block=col_block,
        channels=channels,
    )
    grid_spec = pltpu.PrefetchScalarGridSpec(
        num_scalar_prefetch=3,
        grid=(rows,),
        in_specs=[
            pl.BlockSpec((1, ext_views, 1, width), lambda r, *_: (r, 0, 0, 0)),
            pl.BlockSpec((channels, 16), lambda r, *_: (0, 0)),
            pl.BlockSpec((channels, 9 * channels), lambda r, *_: (0, 0)),
            pl.BlockSpec((channels, 1), lambda r, *_: (0, 0)),
        ],
        out_specs=pl.BlockSpec((1, out_views, width), lambda r, *_: (r, 0, 0)),
        scratch_shapes=[
            pltpu.VMEM((pad_rows, width), jnp.float32),
            pltpu.VMEM((first_views * 3 * channels, width), jnp.bfloat16),
            pltpu.VMEM((out_views, width), jnp.float32),
        ],
    )
    return pl.pallas_call(
        kernel,
        out_shape=jax.ShapeDtypeStruct((rows, out_views, width), jnp.bfloat16),
        grid_spec=grid_spec,
    )(
        offsets.reshape(-1),
        weights.reshape(-1),
        bounds,
        extended.astype(jnp.float32).reshape(rows, ext_views, 1, width),
        w1.astype(jnp.bfloat16),
        w2.astype(jnp.bfloat16),
        kl,
    )


def prepare(mantissa, exponent, poly_square, poly_cube):
    lead_rows, lead_views, width_all = mantissa.shape
    block_count = exponent.shape[2]
    counts = mantissa.astype(jnp.float32).reshape(
        lead_rows, lead_views, block_count, width_all // block_count
    )
    counts = counts * jnp.exp2(-exponent.astype(jnp.float32))[..., None]
    line_int = -jnp.log(counts).reshape(lead_rows, lead_views, width_all)
    hardened = (
        line_int + poly_square * line_int * line_int + poly_cube * line_int * line_int * line_int
    )
    return hardened.astype(jnp.bfloat16)


def resample(hardened, col_map):
    shape_in = hardened.shape
    flat = hardened.reshape(-1, shape_in[2])
    product = jnp.dot(flat, col_map, preferred_element_type=jnp.float32)
    return product.astype(jnp.bfloat16).reshape(shape_in)


def local(
    mantissa,
    exponent,
    poly_square,
    poly_cube,
    col_map,
    rebin_offset,
    rebin_weight,
    kern_first,
    kern_second,
    kern_last,
):
    projected = resample(prepare(mantissa, exponent, poly_square, poly_cube), col_map)
    row_major = lax.all_to_all(projected, "dev", split_axis=0, concat_axis=1, tiled=True)
    row_count, view_count = (row_major.shape[0], row_major.shape[1])
    group_idx = lax.axis_index("group")
    total_views = view_count * lax.axis_size("group")
    view_start = group_idx * view_count
    halo = REACH + RIM

    params = jnp.stack([rebin_offset.astype(jnp.float32), rebin_weight], axis=0)
    low, high = halo_exchange(row_major, "group", 1, halo)
    params_low, params_high = halo_exchange(params, "group", 1, RIM)
    extended = jnp.concatenate([low, row_major, high], axis=1)
    params_ext = jnp.concatenate([params_low, params, params_high], axis=1)

    offsets = params_ext[0].astype(jnp.int32)
    weights = params_ext[1]
    bounds = jnp.stack([view_start, total_views]).astype(jnp.int32)
    return rebin_dual(extended, offsets, weights, bounds, kern_first, kern_second, kern_last)


def solution(mesh):
    return jax.shard_map(
        local,
        mesh=mesh,
        in_specs=(
            P(None, ("group", "dev"), None),
            P(None, ("group", "dev"), None),
            P(),
            P(),
            P(),
            P("group", None),
            P("group", None),
            P(),
            P(),
            P(),
        ),
        out_specs=P("dev", "group", None),
        check_vma=False,
    )
```

```python
import functools

import jax
import jax.numpy as jnp
from jax import lax
from jax.experimental import pallas as pl
from jax.experimental.pallas import tpu as pltpu
from jax.sharding import PartitionSpec as P

REACH = 8
RIM = 2


def conv_kernel(
    offset_ref,
    weight_ref,
    bounds_ref,
    ext_ref,
    w1_ref,
    w2_ref,
    kl_ref,
    out_ref,
    sig_ref,
    feat_ref,
    dual_ref,
    *,
    sig_views,
    block_count,
    col_block,
    channels,
):
    width = block_count * col_block
    first_views = sig_views - 2
    out_views = sig_views - 4
    view_start = bounds_ref[0]
    total_views = bounds_ref[1]
    lane = lax.broadcasted_iota(jnp.int32, (1, width), 1)
    sig_ref[3 * sig_views :, :] = jnp.zeros((sig_ref.shape[0] - 3 * sig_views, width), jnp.float32)
    for u in range(sig_views):
        pos = view_start - RIM + u
        keep = ((pos >= 0) & (pos < total_views)).astype(jnp.float32)
        for k in range(block_count):
            low = u + offset_ref[u * block_count + k] + REACH
            frac = weight_ref[u * block_count + k]
            cols = pl.ds(k * col_block, col_block)
            lower = ext_ref[0, low, :, cols]
            upper = ext_ref[0, low + 1, :, cols]
            value = ((1.0 - frac) * lower + frac * upper).astype(jnp.bfloat16)
            sig_ref[3 * u + 1 : 3 * u + 2, cols] = value.astype(jnp.float32) * keep
        row = sig_ref[3 * u + 1 : 3 * u + 2, :]
        sig_ref[3 * u : 3 * u + 1, :] = jnp.where(lane >= 1, pltpu.roll(row, 1, 1), 0.0)
        sig_ref[3 * u + 2 : 3 * u + 3, :] = jnp.where(
            lane < width - 1, pltpu.roll(row, width - 1, 1), 0.0
        )
    col = lax.broadcasted_iota(jnp.int32, (channels, width), 1)
    keep_left = col >= 1
    keep_right = col < width - 1
    w1 = w1_ref[...]
    for u in range(first_views):
        taps = sig_ref[3 * u : 3 * u + 16, :].astype(jnp.bfloat16)
        hidden = jnp.dot(w1, taps, preferred_element_type=jnp.float32)
        pos = view_start - 1 + u
        scale = ((pos >= 0) & (pos < total_views)).astype(jnp.float32)
        hidden = jnp.maximum(hidden, 0.0) * scale
        base = 3 * u * channels
        feat_ref[base : base + channels, :] = jnp.where(
            keep_left, pltpu.roll(hidden, 1, 1), 0.0
        ).astype(jnp.bfloat16)
        feat_ref[base + channels : base + 2 * channels, :] = hidden.astype(jnp.bfloat16)
        feat_ref[base + 2 * channels : base + 3 * channels, :] = jnp.where(
            keep_right, pltpu.roll(hidden, width - 1, 1), 0.0
        ).astype(jnp.bfloat16)
    w2 = w2_ref[...]
    kl = kl_ref[...]
    for v in range(out_views):
        window = feat_ref[3 * v * channels : 3 * (v + 3) * channels, :]
        second = jnp.dot(w2, window, preferred_element_type=jnp.float32)
        second = jnp.maximum(second, 0.0).astype(jnp.bfloat16).astype(jnp.float32)
        mix = jnp.sum(kl * second, axis=0, keepdims=True)
        centre = sig_ref[3 * (v + 2) + 1 : 3 * (v + 2) + 2, :]
        dual_ref[v : v + 1, :] = centre + mix
    out_ref[0] = dual_ref[...].astype(out_ref.dtype)


def rebin_dual(extended, offsets, weights, bounds, kern_first, kern_second, kern_last):
    rows, ext_views, width = extended.shape
    sig_views, block_count = offsets.shape
    col_block = width // block_count
    channels = kern_first.shape[0]
    first_views = sig_views - 2
    out_views = sig_views - 4
    pad_rows = -(-(3 * first_views + 13) // 8) * 8
    w1 = jnp.pad(kern_first.reshape(channels, 9), ((0, 0), (0, 7)))
    w2 = jnp.transpose(kern_second, (0, 2, 3, 1)).reshape(channels, 9 * channels)
    kl = kern_last.astype(jnp.float32).reshape(channels, 1)
    kernel = functools.partial(
        conv_kernel,
        sig_views=sig_views,
        block_count=block_count,
        col_block=col_block,
        channels=channels,
    )
    grid_spec = pltpu.PrefetchScalarGridSpec(
        num_scalar_prefetch=3,
        grid=(rows,),
        in_specs=[
            pl.BlockSpec((1, ext_views, 1, width), lambda r, *_: (r, 0, 0, 0)),
            pl.BlockSpec((channels, 16), lambda r, *_: (0, 0)),
            pl.BlockSpec((channels, 9 * channels), lambda r, *_: (0, 0)),
            pl.BlockSpec((channels, 1), lambda r, *_: (0, 0)),
        ],
        out_specs=pl.BlockSpec((1, out_views, width), lambda r, *_: (r, 0, 0)),
        scratch_shapes=[
            pltpu.VMEM((pad_rows, width), jnp.float32),
            pltpu.VMEM((first_views * 3 * channels, width), jnp.bfloat16),
            pltpu.VMEM((out_views, width), jnp.float32),
        ],
    )
    return pl.pallas_call(
        kernel,
        out_shape=jax.ShapeDtypeStruct((rows, out_views, width), jnp.bfloat16),
        grid_spec=grid_spec,
    )(
        offsets.reshape(-1),
        weights.reshape(-1),
        bounds,
        extended.astype(jnp.float32).reshape(rows, ext_views, 1, width),
        w1.astype(jnp.bfloat16),
        w2.astype(jnp.bfloat16),
        kl,
    )


def prepare(mantissa, exponent, poly_square, poly_cube):
    lead_rows, lead_views, width_all = mantissa.shape
    block_count = exponent.shape[2]
    counts = mantissa.astype(jnp.float32).reshape(
        lead_rows, lead_views, block_count, width_all // block_count
    )
    counts = counts * jnp.exp2(-exponent.astype(jnp.float32))[..., None]
    line_int = -jnp.log(counts).reshape(lead_rows, lead_views, width_all)
    hardened = (
        line_int + poly_square * line_int * line_int + poly_cube * line_int * line_int * line_int
    )
    return hardened.astype(jnp.bfloat16)


def resample(hardened, col_map):
    shape_in = hardened.shape
    flat = hardened.reshape(-1, shape_in[2])
    product = jnp.dot(flat, col_map, preferred_element_type=jnp.float32)
    return product.astype(jnp.bfloat16).reshape(shape_in)


def local(
    mantissa,
    exponent,
    poly_square,
    poly_cube,
    col_map,
    rebin_offset,
    rebin_weight,
    kern_first,
    kern_second,
    kern_last,
):
    projected = resample(prepare(mantissa, exponent, poly_square, poly_cube), col_map)
    lead_rows, _, width = projected.shape
    group_count = lax.axis_size("group")
    dev_count = lax.axis_size("dev")
    row_count = lead_rows // dev_count
    block_count = rebin_offset.shape[1]
    view_count = rebin_offset.shape[0]
    total_views = view_count * group_count
    view_start = lax.axis_index("group") * view_count

    own = lax.axis_index("dev")
    own_offset = lax.dynamic_slice_in_dim(rebin_offset, own, 1, axis=0).astype(jnp.float32)
    own_weight = lax.dynamic_slice_in_dim(rebin_weight, own, 1, axis=0)
    weight_high = lax.reduce_precision(own_weight, exponent_bits=8, mantissa_bits=7)
    rest = own_weight - weight_high
    weight_mid = lax.reduce_precision(rest, exponent_bits=8, mantissa_bits=7)
    weight_low = rest - weight_mid
    param_row = jnp.concatenate([own_offset, weight_high, weight_mid, weight_low], axis=1)
    param_row = param_row.astype(jnp.bfloat16)
    param_row = jnp.pad(param_row, ((0, 0), (0, width - 4 * block_count)))
    chunk = jnp.concatenate(
        [
            projected.reshape(dev_count, row_count, width),
            jnp.broadcast_to(param_row[None], (dev_count, 1, width)),
        ],
        axis=1,
    )
    chunk = jnp.broadcast_to(chunk[None], (group_count,) + chunk.shape)
    chunk = chunk.reshape(group_count * dev_count, row_count + 1, width)
    received = lax.all_to_all(chunk, ("group", "dev"), 0, 0, tiled=True)

    halo = REACH + RIM
    views = jnp.pad(received[:, :row_count], ((halo, halo), (0, 0), (0, 0)))
    views = lax.dynamic_slice_in_dim(views, view_start, view_count + 2 * halo, axis=0)
    extended = jnp.transpose(views, (1, 0, 2))
    params = received[:, row_count, : 4 * block_count].astype(jnp.float32)
    params = jnp.pad(params, ((RIM, RIM), (0, 0)))
    params = lax.dynamic_slice_in_dim(params, view_start, view_count + 2 * RIM, axis=0)
    offsets = params[:, :block_count].astype(jnp.int32)
    weights = params[:, block_count : 2 * block_count] + (
        params[:, 2 * block_count : 3 * block_count] + params[:, 3 * block_count :]
    )
    bounds = jnp.stack([view_start, total_views]).astype(jnp.int32)
    return rebin_dual(extended, offsets, weights, bounds, kern_first, kern_second, kern_last)


def solution(mesh):
    return jax.shard_map(
        local,
        mesh=mesh,
        in_specs=(
            P(None, ("group", "dev"), None),
            P(None, ("group", "dev"), None),
            P(),
            P(),
            P(),
            P("group", None),
            P("group", None),
            P(),
            P(),
            P(),
        ),
        out_specs=P("dev", "group", None),
        check_vma=False,
    )
```

```python
import functools

import jax
import jax.numpy as jnp
from jax import lax
from jax.experimental import pallas as pl
from jax.experimental.pallas import tpu as pltpu
from jax.sharding import PartitionSpec as P

REACH = 8
RIM = 2


def conv_kernel(
    offset_ref,
    weight_ref,
    bounds_ref,
    ext_ref,
    w1_ref,
    w2_ref,
    kl_ref,
    out_ref,
    sig_ref,
    feat_ref,
    dual_ref,
    *,
    sig_views,
    block_count,
    col_block,
    channels,
):
    width = block_count * col_block
    first_views = sig_views - 2
    out_views = sig_views - 4
    view_start = bounds_ref[0]
    total_views = bounds_ref[1]
    lane = lax.broadcasted_iota(jnp.int32, (1, width), 1)
    sig_ref[3 * sig_views :, :] = jnp.zeros((sig_ref.shape[0] - 3 * sig_views, width), jnp.float32)
    for u in range(sig_views):
        pos = view_start - RIM + u
        keep = ((pos >= 0) & (pos < total_views)).astype(jnp.float32)
        for k in range(block_count):
            low = u + offset_ref[u * block_count + k] + REACH
            frac = weight_ref[u * block_count + k]
            cols = pl.ds(k * col_block, col_block)
            lower = ext_ref[0, low, :, cols]
            upper = ext_ref[0, low + 1, :, cols]
            value = ((1.0 - frac) * lower + frac * upper).astype(jnp.bfloat16)
            sig_ref[3 * u + 1 : 3 * u + 2, cols] = value.astype(jnp.float32) * keep
        row = sig_ref[3 * u + 1 : 3 * u + 2, :]
        sig_ref[3 * u : 3 * u + 1, :] = jnp.where(lane >= 1, pltpu.roll(row, 1, 1), 0.0)
        sig_ref[3 * u + 2 : 3 * u + 3, :] = jnp.where(
            lane < width - 1, pltpu.roll(row, width - 1, 1), 0.0
        )
    col = lax.broadcasted_iota(jnp.int32, (channels, width), 1)
    keep_left = col >= 1
    keep_right = col < width - 1
    w1 = w1_ref[...]
    for u in range(first_views):
        taps = sig_ref[3 * u : 3 * u + 16, :].astype(jnp.bfloat16)
        hidden = jnp.dot(w1, taps, preferred_element_type=jnp.float32)
        pos = view_start - 1 + u
        scale = ((pos >= 0) & (pos < total_views)).astype(jnp.float32)
        hidden = jnp.maximum(hidden, 0.0) * scale
        base = 3 * u * channels
        feat_ref[base : base + channels, :] = jnp.where(
            keep_left, pltpu.roll(hidden, 1, 1), 0.0
        ).astype(jnp.bfloat16)
        feat_ref[base + channels : base + 2 * channels, :] = hidden.astype(jnp.bfloat16)
        feat_ref[base + 2 * channels : base + 3 * channels, :] = jnp.where(
            keep_right, pltpu.roll(hidden, width - 1, 1), 0.0
        ).astype(jnp.bfloat16)
    w2 = w2_ref[...]
    kl = kl_ref[...]
    for v in range(out_views):
        window = feat_ref[3 * v * channels : 3 * (v + 3) * channels, :]
        second = jnp.dot(w2, window, preferred_element_type=jnp.float32)
        second = jnp.maximum(second, 0.0).astype(jnp.bfloat16).astype(jnp.float32)
        mix = jnp.sum(kl * second, axis=0, keepdims=True)
        centre = sig_ref[3 * (v + 2) + 1 : 3 * (v + 2) + 2, :]
        dual_ref[v : v + 1, :] = centre + mix
    out_ref[0] = dual_ref[...].astype(out_ref.dtype)


def rebin_dual(extended, offsets, weights, bounds, kern_first, kern_second, kern_last):
    rows, ext_views, width = extended.shape
    sig_views, block_count = offsets.shape
    col_block = width // block_count
    channels = kern_first.shape[0]
    first_views = sig_views - 2
    out_views = sig_views - 4
    pad_rows = -(-(3 * first_views + 13) // 8) * 8
    w1 = jnp.pad(kern_first.reshape(channels, 9), ((0, 0), (0, 7)))
    w2 = jnp.transpose(kern_second, (0, 2, 3, 1)).reshape(channels, 9 * channels)
    kl = kern_last.astype(jnp.float32).reshape(channels, 1)
    kernel = functools.partial(
        conv_kernel,
        sig_views=sig_views,
        block_count=block_count,
        col_block=col_block,
        channels=channels,
    )
    grid_spec = pltpu.PrefetchScalarGridSpec(
        num_scalar_prefetch=3,
        grid=(rows,),
        in_specs=[
            pl.BlockSpec((1, ext_views, 1, width), lambda r, *_: (r, 0, 0, 0)),
            pl.BlockSpec((channels, 16), lambda r, *_: (0, 0)),
            pl.BlockSpec((channels, 9 * channels), lambda r, *_: (0, 0)),
            pl.BlockSpec((channels, 1), lambda r, *_: (0, 0)),
        ],
        out_specs=pl.BlockSpec((1, out_views, width), lambda r, *_: (r, 0, 0)),
        scratch_shapes=[
            pltpu.VMEM((pad_rows, width), jnp.float32),
            pltpu.VMEM((first_views * 3 * channels, width), jnp.bfloat16),
            pltpu.VMEM((out_views, width), jnp.float32),
        ],
    )
    return pl.pallas_call(
        kernel,
        out_shape=jax.ShapeDtypeStruct((rows, out_views, width), jnp.bfloat16),
        grid_spec=grid_spec,
    )(
        offsets.reshape(-1),
        weights.reshape(-1),
        bounds,
        extended.astype(jnp.float32).reshape(rows, ext_views, 1, width),
        w1.astype(jnp.bfloat16),
        w2.astype(jnp.bfloat16),
        kl,
    )


def prepare(mantissa, exponent, poly_square, poly_cube):
    lead_rows, lead_views, width_all = mantissa.shape
    block_count = exponent.shape[2]
    counts = mantissa.astype(jnp.float32).reshape(
        lead_rows, lead_views, block_count, width_all // block_count
    )
    counts = counts * jnp.exp2(-exponent.astype(jnp.float32))[..., None]
    line_int = -jnp.log(counts).reshape(lead_rows, lead_views, width_all)
    hardened = (
        line_int + poly_square * line_int * line_int + poly_cube * line_int * line_int * line_int
    )
    return hardened.astype(jnp.bfloat16)


def resample(hardened, col_map):
    shape_in = hardened.shape
    flat = hardened.reshape(-1, shape_in[2])
    product = jnp.dot(flat, col_map, preferred_element_type=jnp.float32)
    return product.astype(jnp.bfloat16).reshape(shape_in)


def local(
    mantissa,
    exponent,
    poly_square,
    poly_cube,
    col_map,
    rebin_offset,
    rebin_weight,
    kern_first,
    kern_second,
    kern_last,
):
    projected = resample(prepare(mantissa, exponent, poly_square, poly_cube), col_map)
    lead_rows, _, width = projected.shape
    group_count = lax.axis_size("group")
    dev_count = lax.axis_size("dev")
    row_count = lead_rows // dev_count
    block_count = rebin_offset.shape[1]
    view_count = rebin_offset.shape[0]
    total_views = view_count * group_count
    view_start = lax.axis_index("group") * view_count

    weight_high = lax.reduce_precision(rebin_weight, exponent_bits=8, mantissa_bits=7)
    rest = rebin_weight - weight_high
    weight_mid = lax.reduce_precision(rest, exponent_bits=8, mantissa_bits=7)
    weight_low = rest - weight_mid
    param_block = jnp.concatenate(
        [rebin_offset.astype(jnp.float32), weight_high, weight_mid, weight_low], axis=1
    )
    param_size = view_count * 4 * block_count
    param_rows = -(-param_size // width)
    param_block = jnp.pad(param_block.reshape(-1), (0, param_rows * width - param_size))
    param_block = param_block.astype(jnp.bfloat16).reshape(1, param_rows, width)

    pieces = 1
    piece_rows = row_count // pieces
    by_dest = projected.reshape(dev_count, row_count, width)
    halo = REACH + RIM
    outputs = []
    params = None
    for piece in range(pieces):
        part = by_dest[:, piece * piece_rows : (piece + 1) * piece_rows]
        if piece == 0:
            part = jnp.concatenate(
                [part, jnp.broadcast_to(param_block, (dev_count, param_rows, width))], axis=1
            )
        part = jnp.broadcast_to(part[None], (group_count,) + part.shape)
        part = part.reshape((group_count * dev_count,) + part.shape[2:])
        received = lax.all_to_all(part, ("group", "dev"), 0, 0, tiled=True)
        if piece == 0:
            table = received.reshape(group_count, dev_count, -1, width)[:, 0, piece_rows:]
            table = table.reshape(group_count, -1)[:, :param_size].astype(jnp.float32)
            table = table.reshape(total_views, 4 * block_count)
            table = jnp.pad(table, ((RIM, RIM), (0, 0)))
            params = lax.dynamic_slice_in_dim(table, view_start, view_count + 2 * RIM, axis=0)
        views = jnp.pad(received[:, :piece_rows], ((halo, halo), (0, 0), (0, 0)))
        views = lax.dynamic_slice_in_dim(views, view_start, view_count + 2 * halo, axis=0)
        extended = jnp.transpose(views, (1, 0, 2))
        offsets = params[:, :block_count].astype(jnp.int32)
        weights = params[:, block_count : 2 * block_count] + (
            params[:, 2 * block_count : 3 * block_count] + params[:, 3 * block_count :]
        )
        bounds = jnp.stack([view_start, total_views]).astype(jnp.int32)
        outputs.append(
            rebin_dual(extended, offsets, weights, bounds, kern_first, kern_second, kern_last)
        )
    return jnp.concatenate(outputs, axis=0) if pieces > 1 else outputs[0]


def solution(mesh):
    return jax.shard_map(
        local,
        mesh=mesh,
        in_specs=(
            P(None, ("group", "dev"), None),
            P(None, ("group", "dev"), None),
            P(),
            P(),
            P(),
            P("group", None),
            P("group", None),
            P(),
            P(),
            P(),
        ),
        out_specs=P("dev", "group", None),
        check_vma=False,
    )
```

```python
import functools

import jax
import jax.numpy as jnp
from jax import lax
from jax.experimental import pallas as pl
from jax.experimental.pallas import tpu as pltpu
from jax.sharding import PartitionSpec as P

REACH = 8
RIM = 2


def conv_kernel(
    offset_ref,
    weight_ref,
    bounds_ref,
    ext_ref,
    w1_ref,
    w2_ref,
    kl_ref,
    out_ref,
    sig_ref,
    feat_ref,
    dual_ref,
    *,
    sig_views,
    block_count,
    col_block,
    channels,
    fold,
):
    width = block_count * col_block
    rows = sig_ref.shape[0]
    first_views = sig_views - 2
    out_views = sig_views - 4
    view_start = bounds_ref[0]
    total_views = bounds_ref[1]
    row = pl.program_id(0)

    @pl.when(row == 0)
    def _rebin():
        lane = lax.broadcasted_iota(jnp.int32, (1, width), 1)
        pad = sig_ref.shape[1] - 3 * sig_views
        for r in range(rows):
            sig_ref[r, 3 * sig_views :, :] = jnp.zeros((pad, width), jnp.float32)

        def pick(view, cols):
            tile = ext_ref[view // fold, :, cols]
            part = view % fold
            picked = tile[0:rows]
            for f in range(1, fold):
                picked = jnp.where(part == f, tile[f * rows : (f + 1) * rows], picked)
            return picked

        for u in range(sig_views):
            pos = view_start - RIM + u
            keep = ((pos >= 0) & (pos < total_views)).astype(jnp.float32)
            for k in range(block_count):
                low = u + offset_ref[u * block_count + k] + REACH
                frac = weight_ref[u * block_count + k]
                cols = pl.ds(k * col_block, col_block)
                lower = pick(low, cols)
                upper = pick(low + 1, cols)
                value = ((1.0 - frac) * lower + frac * upper).astype(jnp.bfloat16)
                value = value.astype(jnp.float32) * keep
                for r in range(rows):
                    sig_ref[r, 3 * u + 1 : 3 * u + 2, cols] = value[r : r + 1]
            for r in range(rows):
                line = sig_ref[r, 3 * u + 1 : 3 * u + 2, :]
                sig_ref[r, 3 * u : 3 * u + 1, :] = jnp.where(lane >= 1, pltpu.roll(line, 1, 1), 0.0)
                sig_ref[r, 3 * u + 2 : 3 * u + 3, :] = jnp.where(
                    lane < width - 1, pltpu.roll(line, width - 1, 1), 0.0
                )

    col = lax.broadcasted_iota(jnp.int32, (channels, width), 1)
    keep_left = col >= 1
    keep_right = col < width - 1
    zero = jnp.zeros((channels, width), jnp.bfloat16)
    w1 = w1_ref[...]
    for u in range(first_views):
        taps = sig_ref[row, 3 * u : 3 * u + 16, :].astype(jnp.bfloat16)
        hidden = jnp.dot(w1, taps, preferred_element_type=jnp.float32)
        pos = view_start - 1 + u
        scale = ((pos >= 0) & (pos < total_views)).astype(jnp.float32)
        hidden = (jnp.maximum(hidden, 0.0) * scale).astype(jnp.bfloat16)
        base = 3 * u * channels
        feat_ref[base : base + channels, :] = jnp.where(keep_left, pltpu.roll(hidden, 1, 1), zero)
        feat_ref[base + channels : base + 2 * channels, :] = hidden
        feat_ref[base + 2 * channels : base + 3 * channels, :] = jnp.where(
            keep_right, pltpu.roll(hidden, width - 1, 1), zero
        )
    w2 = w2_ref[...]
    kl = kl_ref[...]
    for v in range(out_views):
        window = feat_ref[3 * v * channels : 3 * (v + 3) * channels, :]
        second = jnp.dot(w2, window, preferred_element_type=jnp.float32)
        second = jnp.maximum(second, 0.0).astype(jnp.bfloat16).astype(jnp.float32)
        mix = jnp.sum(kl * second, axis=0, keepdims=True)
        centre = sig_ref[row, 3 * (v + 2) + 1 : 3 * (v + 2) + 2, :]
        dual_ref[v : v + 1, :] = centre + mix
    out_ref[0] = dual_ref[...].astype(out_ref.dtype)


def rebin_dual(views, offsets, weights, bounds, kern_first, kern_second, kern_last):
    ext_views, rows, width = views.shape
    sig_views, block_count = offsets.shape
    col_block = width // block_count
    channels = kern_first.shape[0]
    first_views = sig_views - 2
    out_views = sig_views - 4
    fold = 8 // rows if 8 % rows == 0 else 1
    tiles = -(-ext_views // fold)
    views = jnp.pad(views, ((0, tiles * fold - ext_views), (0, 0), (0, 0)))
    ext = views.astype(jnp.float32).reshape(tiles, fold * rows, width)
    pad_rows = -(-(3 * first_views + 13) // 8) * 8
    w1 = jnp.pad(kern_first.reshape(channels, 9), ((0, 0), (0, 7)))
    w2 = jnp.transpose(kern_second, (0, 2, 3, 1)).reshape(channels, 9 * channels)
    kl = kern_last.astype(jnp.float32).reshape(channels, 1)
    kernel = functools.partial(
        conv_kernel,
        sig_views=sig_views,
        block_count=block_count,
        col_block=col_block,
        channels=channels,
        fold=fold,
    )
    grid_spec = pltpu.PrefetchScalarGridSpec(
        num_scalar_prefetch=3,
        grid=(rows,),
        in_specs=[
            pl.BlockSpec((tiles, fold * rows, width), lambda r, *_: (0, 0, 0)),
            pl.BlockSpec((channels, 16), lambda r, *_: (0, 0)),
            pl.BlockSpec((channels, 9 * channels), lambda r, *_: (0, 0)),
            pl.BlockSpec((channels, 1), lambda r, *_: (0, 0)),
        ],
        out_specs=pl.BlockSpec((1, out_views, width), lambda r, *_: (r, 0, 0)),
        scratch_shapes=[
            pltpu.VMEM((rows, pad_rows, width), jnp.float32),
            pltpu.VMEM((first_views * 3 * channels, width), jnp.bfloat16),
            pltpu.VMEM((out_views, width), jnp.float32),
        ],
    )
    return pl.pallas_call(
        kernel,
        out_shape=jax.ShapeDtypeStruct((rows, out_views, width), jnp.bfloat16),
        grid_spec=grid_spec,
        compiler_params=pltpu.CompilerParams(dimension_semantics=("arbitrary",)),
    )(
        offsets.reshape(-1),
        weights.reshape(-1),
        bounds,
        ext,
        w1.astype(jnp.bfloat16),
        w2.astype(jnp.bfloat16),
        kl,
    )


def prepare(mantissa, exponent, poly_square, poly_cube):
    lead_rows, lead_views, width_all = mantissa.shape
    block_count = exponent.shape[2]
    counts = mantissa.astype(jnp.float32).reshape(
        lead_rows, lead_views, block_count, width_all // block_count
    )
    counts = counts * jnp.exp2(-exponent.astype(jnp.float32))[..., None]
    line_int = -jnp.log(counts).reshape(lead_rows, lead_views, width_all)
    hardened = (
        line_int + poly_square * line_int * line_int + poly_cube * line_int * line_int * line_int
    )
    return hardened.astype(jnp.bfloat16)


def resample(hardened, col_map):
    shape_in = hardened.shape
    flat = hardened.reshape(-1, shape_in[2])
    product = jnp.dot(flat, col_map, preferred_element_type=jnp.float32)
    return product.astype(jnp.bfloat16).reshape(shape_in)


def local(
    mantissa,
    exponent,
    poly_square,
    poly_cube,
    col_map,
    rebin_offset,
    rebin_weight,
    kern_first,
    kern_second,
    kern_last,
):
    projected = resample(prepare(mantissa, exponent, poly_square, poly_cube), col_map)
    lead_rows, _, width = projected.shape
    group_count = lax.axis_size("group")
    dev_count = lax.axis_size("dev")
    row_count = lead_rows // dev_count
    block_count = rebin_offset.shape[1]
    view_count = rebin_offset.shape[0]
    total_views = view_count * group_count
    view_start = lax.axis_index("group") * view_count

    weight_high = lax.reduce_precision(rebin_weight, exponent_bits=8, mantissa_bits=7)
    rest = rebin_weight - weight_high
    weight_mid = lax.reduce_precision(rest, exponent_bits=8, mantissa_bits=7)
    weight_low = rest - weight_mid
    param_block = jnp.concatenate(
        [rebin_offset.astype(jnp.float32), weight_high, weight_mid, weight_low], axis=1
    )
    param_size = view_count * 4 * block_count
    param_rows = -(-param_size // width)
    param_block = jnp.pad(param_block.reshape(-1), (0, param_rows * width - param_size))
    param_block = param_block.astype(jnp.bfloat16).reshape(1, param_rows, width)

    pieces = 1
    piece_rows = row_count // pieces
    by_dest = projected.reshape(dev_count, row_count, width)
    halo = REACH + RIM
    outputs = []
    params = None
    for piece in range(pieces):
        part = by_dest[:, piece * piece_rows : (piece + 1) * piece_rows]
        if piece == 0:
            part = jnp.concatenate(
                [part, jnp.broadcast_to(param_block, (dev_count, param_rows, width))], axis=1
            )
        part = jnp.broadcast_to(part[None], (group_count,) + part.shape)
        part = part.reshape((group_count * dev_count,) + part.shape[2:])
        received = lax.all_to_all(part, ("group", "dev"), 0, 0, tiled=True)
        if piece == 0:
            table = received.reshape(group_count, dev_count, -1, width)[:, 0, piece_rows:]
            table = table.reshape(group_count, -1)[:, :param_size].astype(jnp.float32)
            table = table.reshape(total_views, 4 * block_count)
            table = jnp.pad(table, ((RIM, RIM), (0, 0)))
            params = lax.dynamic_slice_in_dim(table, view_start, view_count + 2 * RIM, axis=0)
        views = jnp.pad(received[:, :piece_rows], ((halo, halo), (0, 0), (0, 0)))
        views = lax.dynamic_slice_in_dim(views, view_start, view_count + 2 * halo, axis=0)
        offsets = params[:, :block_count].astype(jnp.int32)
        weights = params[:, block_count : 2 * block_count] + (
            params[:, 2 * block_count : 3 * block_count] + params[:, 3 * block_count :]
        )
        bounds = jnp.stack([view_start, total_views]).astype(jnp.int32)
        outputs.append(
            rebin_dual(views, offsets, weights, bounds, kern_first, kern_second, kern_last)
        )
    return jnp.concatenate(outputs, axis=0) if pieces > 1 else outputs[0]


def solution(mesh):
    return jax.shard_map(
        local,
        mesh=mesh,
        in_specs=(
            P(None, ("group", "dev"), None),
            P(None, ("group", "dev"), None),
            P(),
            P(),
            P(),
            P("group", None),
            P("group", None),
            P(),
            P(),
            P(),
        ),
        out_specs=P("dev", "group", None),
        check_vma=False,
    )
```

```python
import functools

import jax
import jax.numpy as jnp
from jax import lax
from jax.experimental import pallas as pl
from jax.experimental.pallas import tpu as pltpu
from jax.sharding import PartitionSpec as P

REACH = 8
RIM = 2


def conv_kernel(
    offset_ref,
    weight_ref,
    bounds_ref,
    ext_ref,
    w1_ref,
    w2_ref,
    kl_ref,
    out_ref,
    sig_ref,
    feat_ref,
    dual_ref,
    *,
    sig_views,
    block_count,
    col_block,
    channels,
):
    width = block_count * col_block
    first_views = sig_views - 2
    out_views = sig_views - 4
    view_start = bounds_ref[0]
    total_views = bounds_ref[1]
    lane = lax.broadcasted_iota(jnp.int32, (1, width), 1)
    sig_ref[3 * sig_views :, :] = jnp.zeros((sig_ref.shape[0] - 3 * sig_views, width), jnp.float32)
    for u in range(sig_views):
        pos = view_start - RIM + u
        keep = ((pos >= 0) & (pos < total_views)).astype(jnp.float32)
        for k in range(block_count):
            low = u + offset_ref[u * block_count + k] + REACH
            frac = weight_ref[u * block_count + k]
            cols = pl.ds(k * col_block, col_block)
            lower = ext_ref[0, low, :, cols]
            upper = ext_ref[0, low + 1, :, cols]
            value = ((1.0 - frac) * lower + frac * upper).astype(jnp.bfloat16)
            sig_ref[3 * u + 1 : 3 * u + 2, cols] = value.astype(jnp.float32) * keep
        row = sig_ref[3 * u + 1 : 3 * u + 2, :]
        sig_ref[3 * u : 3 * u + 1, :] = jnp.where(lane >= 1, pltpu.roll(row, 1, 1), 0.0)
        sig_ref[3 * u + 2 : 3 * u + 3, :] = jnp.where(
            lane < width - 1, pltpu.roll(row, width - 1, 1), 0.0
        )
    col = lax.broadcasted_iota(jnp.int32, (channels, width), 1)
    keep_left = col >= 1
    keep_right = col < width - 1
    w1 = w1_ref[...]
    for u in range(first_views):
        taps = sig_ref[3 * u : 3 * u + 16, :].astype(jnp.bfloat16)
        hidden = jnp.dot(w1, taps, preferred_element_type=jnp.float32)
        pos = view_start - 1 + u
        scale = ((pos >= 0) & (pos < total_views)).astype(jnp.float32)
        hidden = jnp.maximum(hidden, 0.0) * scale
        base = 3 * u * channels
        feat_ref[base : base + channels, :] = jnp.where(
            keep_left, pltpu.roll(hidden, 1, 1), 0.0
        ).astype(jnp.bfloat16)
        feat_ref[base + channels : base + 2 * channels, :] = hidden.astype(jnp.bfloat16)
        feat_ref[base + 2 * channels : base + 3 * channels, :] = jnp.where(
            keep_right, pltpu.roll(hidden, width - 1, 1), 0.0
        ).astype(jnp.bfloat16)
    w2 = w2_ref[...]
    kl = kl_ref[...]
    for v in range(out_views):
        window = feat_ref[3 * v * channels : 3 * (v + 3) * channels, :]
        second = jnp.dot(w2, window, preferred_element_type=jnp.float32)
        second = jnp.maximum(second, 0.0).astype(jnp.bfloat16).astype(jnp.float32)
        mix = jnp.sum(kl * second, axis=0, keepdims=True)
        centre = sig_ref[3 * (v + 2) + 1 : 3 * (v + 2) + 2, :]
        dual_ref[v : v + 1, :] = centre + mix
    out_ref[0] = dual_ref[...].astype(out_ref.dtype)


def rebin_dual(extended, offsets, weights, bounds, kern_first, kern_second, kern_last):
    rows, ext_views, width = extended.shape
    sig_views, block_count = offsets.shape
    col_block = width // block_count
    channels = kern_first.shape[0]
    first_views = sig_views - 2
    out_views = sig_views - 4
    pad_rows = -(-(3 * first_views + 13) // 8) * 8
    w1 = jnp.pad(kern_first.reshape(channels, 9), ((0, 0), (0, 7)))
    w2 = jnp.transpose(kern_second, (0, 2, 3, 1)).reshape(channels, 9 * channels)
    kl = kern_last.astype(jnp.float32).reshape(channels, 1)
    kernel = functools.partial(
        conv_kernel,
        sig_views=sig_views,
        block_count=block_count,
        col_block=col_block,
        channels=channels,
    )
    grid_spec = pltpu.PrefetchScalarGridSpec(
        num_scalar_prefetch=3,
        grid=(rows,),
        in_specs=[
            pl.BlockSpec((1, ext_views, 1, width), lambda r, *_: (r, 0, 0, 0)),
            pl.BlockSpec((channels, 16), lambda r, *_: (0, 0)),
            pl.BlockSpec((channels, 9 * channels), lambda r, *_: (0, 0)),
            pl.BlockSpec((channels, 1), lambda r, *_: (0, 0)),
        ],
        out_specs=pl.BlockSpec((1, out_views, width), lambda r, *_: (r, 0, 0)),
        scratch_shapes=[
            pltpu.VMEM((pad_rows, width), jnp.float32),
            pltpu.VMEM((first_views * 3 * channels, width), jnp.bfloat16),
            pltpu.VMEM((out_views, width), jnp.float32),
        ],
    )
    return pl.pallas_call(
        kernel,
        out_shape=jax.ShapeDtypeStruct((rows, out_views, width), jnp.bfloat16),
        grid_spec=grid_spec,
    )(
        offsets.reshape(-1),
        weights.reshape(-1),
        bounds,
        extended.astype(jnp.float32).reshape(rows, ext_views, 1, width),
        w1.astype(jnp.bfloat16),
        w2.astype(jnp.bfloat16),
        kl,
    )


def prepare(mantissa, exponent, poly_square, poly_cube):
    lead_rows, lead_views, width_all = mantissa.shape
    block_count = exponent.shape[2]
    counts = mantissa.astype(jnp.float32).reshape(
        lead_rows, lead_views, block_count, width_all // block_count
    )
    counts = counts * jnp.exp2(-exponent.astype(jnp.float32))[..., None]
    line_int = -jnp.log(counts).reshape(lead_rows, lead_views, width_all)
    hardened = (
        line_int + poly_square * line_int * line_int + poly_cube * line_int * line_int * line_int
    )
    return hardened.astype(jnp.bfloat16)


def resample(hardened, col_map):
    shape_in = hardened.shape
    flat = hardened.reshape(-1, shape_in[2])
    product = jnp.dot(flat, col_map, preferred_element_type=jnp.float32)
    return product.astype(jnp.bfloat16).reshape(shape_in)


def local(
    mantissa,
    exponent,
    poly_square,
    poly_cube,
    col_map,
    rebin_offset,
    rebin_weight,
    kern_first,
    kern_second,
    kern_last,
):
    projected = resample(prepare(mantissa, exponent, poly_square, poly_cube), col_map)
    lead_rows, _, width = projected.shape
    group_count = lax.axis_size("group")
    dev_count = lax.axis_size("dev")
    row_count = lead_rows // dev_count
    block_count = rebin_offset.shape[1]
    view_count = rebin_offset.shape[0]
    total_views = view_count * group_count
    view_start = lax.axis_index("group") * view_count

    weight_high = lax.reduce_precision(rebin_weight, exponent_bits=8, mantissa_bits=7)
    rest = rebin_weight - weight_high
    weight_mid = lax.reduce_precision(rest, exponent_bits=8, mantissa_bits=7)
    weight_low = rest - weight_mid
    table = jnp.concatenate(
        [rebin_offset.astype(jnp.float32), weight_high, weight_mid, weight_low], axis=1
    )
    halo = REACH + RIM
    row_major = lax.all_to_all(projected, "dev", split_axis=0, concat_axis=1, tiled=True)

    def pack(data, params):
        flat = data.reshape(row_count * data.shape[1], width)
        params = params.reshape(-1)
        param_rows = -(-params.shape[0] // width)
        params = jnp.pad(params, (0, param_rows * width - params.shape[0]))
        params = params.astype(jnp.bfloat16).reshape(param_rows, width)
        return jnp.concatenate([flat, params], axis=0)

    def unpack(block, views_in, params_in):
        data = block[: row_count * views_in].reshape(row_count, views_in, width)
        params = block[row_count * views_in :].reshape(-1)[: params_in * 4 * block_count]
        return data, params.astype(jnp.float32).reshape(params_in, 4 * block_count)

    head = pack(row_major[:, :halo], table[:RIM])
    tail = pack(row_major[:, view_count - halo :], table[view_count - RIM :])
    group_idx = lax.axis_index("group")
    if group_count == 2:
        outgoing = jnp.where(group_idx == 0, tail, head)
        incoming = lax.ppermute(outgoing, "group", [(0, 1), (1, 0)])
        from_low = jnp.where(group_idx == 0, jnp.zeros_like(incoming), incoming)
        from_high = jnp.where(group_idx == 0, incoming, jnp.zeros_like(incoming))
    else:
        forward = [(i, i + 1) for i in range(group_count - 1)]
        backward = [(i + 1, i) for i in range(group_count - 1)]
        from_low = lax.ppermute(tail, "group", forward)
        from_high = lax.ppermute(head, "group", backward)
    low_data, low_params = unpack(from_low, halo, RIM)
    high_data, high_params = unpack(from_high, halo, RIM)
    extended = jnp.concatenate([low_data, row_major, high_data], axis=1)
    params = jnp.concatenate([low_params, table, high_params], axis=0)
    offsets = params[:, :block_count].astype(jnp.int32)
    weights = params[:, block_count : 2 * block_count] + (
        params[:, 2 * block_count : 3 * block_count] + params[:, 3 * block_count :]
    )
    bounds = jnp.stack([view_start, total_views]).astype(jnp.int32)
    return rebin_dual(extended, offsets, weights, bounds, kern_first, kern_second, kern_last)


def solution(mesh):
    return jax.shard_map(
        local,
        mesh=mesh,
        in_specs=(
            P(None, ("group", "dev"), None),
            P(None, ("group", "dev"), None),
            P(),
            P(),
            P(),
            P("group", None),
            P("group", None),
            P(),
            P(),
            P(),
        ),
        out_specs=P("dev", "group", None),
        check_vma=False,
    )
```

```python
import functools

import jax
import jax.numpy as jnp
from jax import lax
from jax.experimental import pallas as pl
from jax.experimental.pallas import tpu as pltpu
from jax.sharding import PartitionSpec as P

REACH = 8
RIM = 2


def conv_kernel(
    table_ref,
    bounds_ref,
    ext_ref,
    w1_ref,
    w2_ref,
    kl_ref,
    out_ref,
    sig_ref,
    feat_ref,
    dual_ref,
    *,
    sig_views,
    block_count,
    col_block,
    channels,
):
    width = block_count * col_block
    first_views = sig_views - 2
    out_views = sig_views - 4
    view_start = bounds_ref[0]
    total_views = bounds_ref[1]
    lane = lax.broadcasted_iota(jnp.int32, (1, width), 1)
    sig_ref[3 * sig_views :, :] = jnp.zeros((sig_ref.shape[0] - 3 * sig_views, width), jnp.float32)
    for u in range(sig_views):
        pos = view_start - RIM + u
        keep = ((pos >= 0) & (pos < total_views)).astype(jnp.float32)
        for k in range(block_count):
            entry = u * 4 * block_count + k
            low = u + table_ref[entry].astype(jnp.int32) + REACH
            frac = table_ref[entry + block_count] + (
                table_ref[entry + 2 * block_count] + table_ref[entry + 3 * block_count]
            )
            cols = pl.ds(k * col_block, col_block)
            lower = ext_ref[0, low, :, cols]
            upper = ext_ref[0, low + 1, :, cols]
            value = ((1.0 - frac) * lower + frac * upper).astype(jnp.bfloat16)
            sig_ref[3 * u + 1 : 3 * u + 2, cols] = value.astype(jnp.float32) * keep
        row = sig_ref[3 * u + 1 : 3 * u + 2, :]
        sig_ref[3 * u : 3 * u + 1, :] = jnp.where(lane >= 1, pltpu.roll(row, 1, 1), 0.0)
        sig_ref[3 * u + 2 : 3 * u + 3, :] = jnp.where(
            lane < width - 1, pltpu.roll(row, width - 1, 1), 0.0
        )
    col = lax.broadcasted_iota(jnp.int32, (channels, width), 1)
    keep_left = col >= 1
    keep_right = col < width - 1
    w1 = w1_ref[...]
    for u in range(first_views):
        taps = sig_ref[3 * u : 3 * u + 16, :].astype(jnp.bfloat16)
        hidden = jnp.dot(w1, taps, preferred_element_type=jnp.float32)
        pos = view_start - 1 + u
        scale = ((pos >= 0) & (pos < total_views)).astype(jnp.float32)
        hidden = jnp.maximum(hidden, 0.0) * scale
        base = 3 * u * channels
        feat_ref[base : base + channels, :] = jnp.where(
            keep_left, pltpu.roll(hidden, 1, 1), 0.0
        ).astype(jnp.bfloat16)
        feat_ref[base + channels : base + 2 * channels, :] = hidden.astype(jnp.bfloat16)
        feat_ref[base + 2 * channels : base + 3 * channels, :] = jnp.where(
            keep_right, pltpu.roll(hidden, width - 1, 1), 0.0
        ).astype(jnp.bfloat16)
    w2 = w2_ref[...]
    kl = kl_ref[...]
    for v in range(out_views):
        window = feat_ref[3 * v * channels : 3 * (v + 3) * channels, :]
        second = jnp.dot(w2, window, preferred_element_type=jnp.float32)
        second = jnp.maximum(second, 0.0).astype(jnp.bfloat16).astype(jnp.float32)
        mix = jnp.sum(kl * second, axis=0, keepdims=True)
        centre = sig_ref[3 * (v + 2) + 1 : 3 * (v + 2) + 2, :]
        dual_ref[v : v + 1, :] = centre + mix
    out_ref[0] = dual_ref[...].astype(out_ref.dtype)


def rebin_dual(extended, table, bounds, kern_first, kern_second, kern_last):
    rows, ext_views, width = extended.shape
    sig_views = table.shape[0]
    block_count = table.shape[1] // 4
    col_block = width // block_count
    channels = kern_first.shape[0]
    first_views = sig_views - 2
    out_views = sig_views - 4
    pad_rows = -(-(3 * first_views + 13) // 8) * 8
    w1 = jnp.pad(kern_first.reshape(channels, 9), ((0, 0), (0, 7)))
    w2 = jnp.transpose(kern_second, (0, 2, 3, 1)).reshape(channels, 9 * channels)
    kl = kern_last.astype(jnp.float32).reshape(channels, 1)
    kernel = functools.partial(
        conv_kernel,
        sig_views=sig_views,
        block_count=block_count,
        col_block=col_block,
        channels=channels,
    )
    grid_spec = pltpu.PrefetchScalarGridSpec(
        num_scalar_prefetch=2,
        grid=(rows,),
        in_specs=[
            pl.BlockSpec((1, ext_views, 1, width), lambda r, *_: (r, 0, 0, 0)),
            pl.BlockSpec((channels, 16), lambda r, *_: (0, 0)),
            pl.BlockSpec((channels, 9 * channels), lambda r, *_: (0, 0)),
            pl.BlockSpec((channels, 1), lambda r, *_: (0, 0)),
        ],
        out_specs=pl.BlockSpec((1, out_views, width), lambda r, *_: (r, 0, 0)),
        scratch_shapes=[
            pltpu.VMEM((pad_rows, width), jnp.float32),
            pltpu.VMEM((first_views * 3 * channels, width), jnp.bfloat16),
            pltpu.VMEM((out_views, width), jnp.float32),
        ],
    )
    return pl.pallas_call(
        kernel,
        out_shape=jax.ShapeDtypeStruct((rows, out_views, width), jnp.bfloat16),
        grid_spec=grid_spec,
    )(
        table.reshape(-1),
        bounds,
        extended.astype(jnp.float32).reshape(rows, ext_views, 1, width),
        w1.astype(jnp.bfloat16),
        w2.astype(jnp.bfloat16),
        kl,
    )


def prepare(mantissa, exponent, poly_square, poly_cube):
    lead_rows, lead_views, width_all = mantissa.shape
    block_count = exponent.shape[2]
    counts = mantissa.astype(jnp.float32).reshape(
        lead_rows, lead_views, block_count, width_all // block_count
    )
    counts = counts * jnp.exp2(-exponent.astype(jnp.float32))[..., None]
    line_int = -jnp.log(counts).reshape(lead_rows, lead_views, width_all)
    hardened = (
        line_int + poly_square * line_int * line_int + poly_cube * line_int * line_int * line_int
    )
    return hardened.astype(jnp.bfloat16)


def resample(hardened, col_map):
    shape_in = hardened.shape
    flat = hardened.reshape(-1, shape_in[2])
    product = jnp.dot(flat, col_map, preferred_element_type=jnp.float32)
    return product.astype(jnp.bfloat16).reshape(shape_in)


def local(
    mantissa,
    exponent,
    poly_square,
    poly_cube,
    col_map,
    rebin_offset,
    rebin_weight,
    kern_first,
    kern_second,
    kern_last,
):
    projected = resample(prepare(mantissa, exponent, poly_square, poly_cube), col_map)
    lead_rows, _, width = projected.shape
    group_count = lax.axis_size("group")
    dev_count = lax.axis_size("dev")
    row_count = lead_rows // dev_count
    block_count = rebin_offset.shape[1]
    view_count = rebin_offset.shape[0]
    total_views = view_count * group_count
    view_start = lax.axis_index("group") * view_count

    weight_high = lax.reduce_precision(rebin_weight, exponent_bits=8, mantissa_bits=7)
    rest = rebin_weight - weight_high
    weight_mid = lax.reduce_precision(rest, exponent_bits=8, mantissa_bits=7)
    weight_low = rest - weight_mid
    table = jnp.concatenate(
        [rebin_offset.astype(jnp.float32), weight_high, weight_mid, weight_low], axis=1
    )
    halo = REACH + RIM
    lead_views = projected.shape[1]
    by_dest = projected.reshape(dev_count, row_count, lead_views, width)
    by_source = lax.all_to_all(by_dest, "dev", 0, 0, tiled=True)
    row_major = jnp.transpose(by_source, (1, 0, 2, 3)).reshape(
        row_count, dev_count * lead_views, width
    )

    def pack(data, params):
        flat = data.reshape(row_count * data.shape[1], width)
        params = params.reshape(-1)
        param_rows = -(-params.shape[0] // width)
        params = jnp.pad(params, (0, param_rows * width - params.shape[0]))
        params = params.astype(jnp.bfloat16).reshape(param_rows, width)
        return jnp.concatenate([flat, params], axis=0)

    def unpack(block, views_in, params_in):
        data = block[: row_count * views_in].reshape(row_count, views_in, width)
        params = block[row_count * views_in :].reshape(-1)[: params_in * 4 * block_count]
        return data, params.astype(jnp.float32).reshape(params_in, 4 * block_count)

    head = pack(row_major[:, :halo], table[:RIM])
    tail = pack(row_major[:, view_count - halo :], table[view_count - RIM :])
    group_idx = lax.axis_index("group")
    if group_count == 2:
        outgoing = jnp.where(group_idx == 0, tail, head)
        incoming = lax.ppermute(outgoing, "group", [(0, 1), (1, 0)])
        from_low = jnp.where(group_idx == 0, jnp.zeros_like(incoming), incoming)
        from_high = jnp.where(group_idx == 0, incoming, jnp.zeros_like(incoming))
    else:
        forward = [(i, i + 1) for i in range(group_count - 1)]
        backward = [(i + 1, i) for i in range(group_count - 1)]
        from_low = lax.ppermute(tail, "group", forward)
        from_high = lax.ppermute(head, "group", backward)
    low_data, low_params = unpack(from_low, halo, RIM)
    high_data, high_params = unpack(from_high, halo, RIM)
    extended = jnp.concatenate([low_data, row_major, high_data], axis=1)
    params = jnp.concatenate([low_params, table, high_params], axis=0)
    bounds = jnp.stack([view_start, total_views]).astype(jnp.int32)
    return rebin_dual(extended, params, bounds, kern_first, kern_second, kern_last)


def solution(mesh):
    return jax.shard_map(
        local,
        mesh=mesh,
        in_specs=(
            P(None, ("group", "dev"), None),
            P(None, ("group", "dev"), None),
            P(),
            P(),
            P(),
            P("group", None),
            P("group", None),
            P(),
            P(),
            P(),
        ),
        out_specs=P("dev", "group", None),
        check_vma=False,
    )
```

```python
import functools

import jax
import jax.numpy as jnp
from jax import lax
from jax.experimental import pallas as pl
from jax.experimental.pallas import tpu as pltpu
from jax.sharding import PartitionSpec as P

REACH = 8
RIM = 2


def conv_kernel(
    table_ref,
    bounds_ref,
    ext_ref,
    w1_ref,
    w2_ref,
    kl_ref,
    out_ref,
    sig_ref,
    feat_ref,
    dual_ref,
    *,
    sig_views,
    block_count,
    col_block,
    channels,
):
    width = block_count * col_block
    first_views = sig_views - 2
    out_views = sig_views - 4
    view_start = bounds_ref[0]
    total_views = bounds_ref[1]
    lane = lax.broadcasted_iota(jnp.int32, (1, width), 1)
    sig_ref[3 * sig_views :, :] = jnp.zeros((sig_ref.shape[0] - 3 * sig_views, width), jnp.float32)
    for u in range(sig_views):
        pos = view_start - RIM + u
        keep = ((pos >= 0) & (pos < total_views)).astype(jnp.float32)
        for k in range(block_count):
            entry = u * 2 * block_count + k
            low = u + table_ref[entry].astype(jnp.int32) + REACH
            frac = table_ref[entry + block_count]
            cols = pl.ds(k * col_block, col_block)
            lower = ext_ref[0, low, :, cols]
            upper = ext_ref[0, low + 1, :, cols]
            value = ((1.0 - frac) * lower + frac * upper).astype(jnp.bfloat16)
            sig_ref[3 * u + 1 : 3 * u + 2, cols] = value.astype(jnp.float32) * keep
        row = sig_ref[3 * u + 1 : 3 * u + 2, :]
        sig_ref[3 * u : 3 * u + 1, :] = jnp.where(lane >= 1, pltpu.roll(row, 1, 1), 0.0)
        sig_ref[3 * u + 2 : 3 * u + 3, :] = jnp.where(
            lane < width - 1, pltpu.roll(row, width - 1, 1), 0.0
        )
    col = lax.broadcasted_iota(jnp.int32, (channels, width), 1)
    keep_left = col >= 1
    keep_right = col < width - 1
    zero = jnp.zeros((channels, width), jnp.bfloat16)
    w1 = w1_ref[...]
    for u in range(first_views):
        taps = sig_ref[3 * u : 3 * u + 16, :].astype(jnp.bfloat16)
        pos = view_start - 1 + u
        scale = ((pos >= 0) & (pos < total_views)).astype(jnp.bfloat16)
        hidden = jnp.dot(w1 * scale, taps, preferred_element_type=jnp.float32)
        hidden = jnp.maximum(hidden, 0.0).astype(jnp.bfloat16)
        base = 3 * u * channels
        feat_ref[base : base + channels, :] = jnp.where(keep_left, pltpu.roll(hidden, 1, 1), zero)
        feat_ref[base + channels : base + 2 * channels, :] = hidden
        feat_ref[base + 2 * channels : base + 3 * channels, :] = jnp.where(
            keep_right, pltpu.roll(hidden, width - 1, 1), zero
        )
    w2 = w2_ref[...]
    kl = kl_ref[...]
    for v in range(out_views):
        window = feat_ref[3 * v * channels : 3 * (v + 3) * channels, :]
        second = jnp.dot(w2, window, preferred_element_type=jnp.float32)
        second = jnp.maximum(second, 0.0).astype(jnp.bfloat16)
        mix = jnp.dot(kl, second, preferred_element_type=jnp.float32)[0:1]
        centre = sig_ref[3 * (v + 2) + 1 : 3 * (v + 2) + 2, :]
        dual_ref[v : v + 1, :] = centre + mix
    out_ref[0] = dual_ref[...].astype(out_ref.dtype)


def rebin_dual(extended, table, bounds, kern_first, kern_second, kern_last):
    rows, ext_views, width = extended.shape
    sig_views = table.shape[0]
    block_count = table.shape[1] // 2
    col_block = width // block_count
    channels = kern_first.shape[0]
    first_views = sig_views - 2
    out_views = sig_views - 4
    pad_rows = -(-(3 * first_views + 13) // 8) * 8
    w1 = jnp.pad(kern_first.reshape(channels, 9), ((0, 0), (0, 7)))
    w2 = jnp.transpose(kern_second, (0, 2, 3, 1)).reshape(channels, 9 * channels)
    kl = jnp.pad(kern_last.reshape(1, channels), ((0, 7), (0, 0)))
    kernel = functools.partial(
        conv_kernel,
        sig_views=sig_views,
        block_count=block_count,
        col_block=col_block,
        channels=channels,
    )
    grid_spec = pltpu.PrefetchScalarGridSpec(
        num_scalar_prefetch=2,
        grid=(rows,),
        in_specs=[
            pl.BlockSpec((1, ext_views, 1, width), lambda r, *_: (r, 0, 0, 0)),
            pl.BlockSpec((channels, 16), lambda r, *_: (0, 0)),
            pl.BlockSpec((channels, 9 * channels), lambda r, *_: (0, 0)),
            pl.BlockSpec((8, channels), lambda r, *_: (0, 0)),
        ],
        out_specs=pl.BlockSpec((1, out_views, width), lambda r, *_: (r, 0, 0)),
        scratch_shapes=[
            pltpu.VMEM((pad_rows, width), jnp.float32),
            pltpu.VMEM((first_views * 3 * channels, width), jnp.bfloat16),
            pltpu.VMEM((out_views, width), jnp.float32),
        ],
    )
    return pl.pallas_call(
        kernel,
        out_shape=jax.ShapeDtypeStruct((rows, out_views, width), jnp.bfloat16),
        grid_spec=grid_spec,
    )(
        table.reshape(-1),
        bounds,
        extended.astype(jnp.float32).reshape(rows, ext_views, 1, width),
        w1.astype(jnp.bfloat16),
        w2.astype(jnp.bfloat16),
        kl,
    )


def prepare(mantissa, exponent, poly_square, poly_cube):
    lead_rows, lead_views, width_all = mantissa.shape
    block_count = exponent.shape[2]
    counts = mantissa.astype(jnp.float32).reshape(
        lead_rows, lead_views, block_count, width_all // block_count
    )
    counts = counts * jnp.exp2(-exponent.astype(jnp.float32))[..., None]
    line_int = -jnp.log(counts).reshape(lead_rows, lead_views, width_all)
    hardened = (
        line_int + poly_square * line_int * line_int + poly_cube * line_int * line_int * line_int
    )
    return hardened.astype(jnp.bfloat16)


def resample(hardened, col_map):
    shape_in = hardened.shape
    flat = hardened.reshape(-1, shape_in[2])
    product = jnp.dot(flat, col_map, preferred_element_type=jnp.float32)
    return product.astype(jnp.bfloat16).reshape(shape_in)


def local(
    mantissa,
    exponent,
    poly_square,
    poly_cube,
    col_map,
    rebin_offset,
    rebin_weight,
    kern_first,
    kern_second,
    kern_last,
):
    projected = resample(prepare(mantissa, exponent, poly_square, poly_cube), col_map)
    lead_rows, _, width = projected.shape
    group_count = lax.axis_size("group")
    dev_count = lax.axis_size("dev")
    row_count = lead_rows // dev_count
    block_count = rebin_offset.shape[1]
    view_count = rebin_offset.shape[0]
    total_views = view_count * group_count
    view_start = lax.axis_index("group") * view_count

    weight_high = lax.reduce_precision(rebin_weight, exponent_bits=8, mantissa_bits=7)
    rest = rebin_weight - weight_high
    weight_mid = lax.reduce_precision(rest, exponent_bits=8, mantissa_bits=7)
    weight_low = rest - weight_mid
    table = jnp.concatenate(
        [rebin_offset.astype(jnp.float32), weight_high, weight_mid, weight_low], axis=1
    )
    halo = REACH + RIM
    lead_views = projected.shape[1]
    by_dest = projected.reshape(dev_count, row_count, lead_views, width)
    by_source = lax.all_to_all(by_dest, "dev", 0, 0, tiled=True)
    row_major = jnp.transpose(by_source, (1, 0, 2, 3)).reshape(
        row_count, dev_count * lead_views, width
    )

    def pack(data, params):
        flat = data.reshape(row_count * data.shape[1], width)
        params = params.reshape(-1)
        param_rows = -(-params.shape[0] // width)
        params = jnp.pad(params, (0, param_rows * width - params.shape[0]))
        params = params.astype(jnp.bfloat16).reshape(param_rows, width)
        return jnp.concatenate([flat, params], axis=0)

    def unpack(block, views_in, params_in):
        data = block[: row_count * views_in].reshape(row_count, views_in, width)
        params = block[row_count * views_in :].reshape(-1)[: params_in * 4 * block_count]
        return data, params.astype(jnp.float32).reshape(params_in, 4 * block_count)

    head = pack(row_major[:, :halo], table[:RIM])
    tail = pack(row_major[:, view_count - halo :], table[view_count - RIM :])
    group_idx = lax.axis_index("group")
    if group_count == 2:
        outgoing = jnp.where(group_idx == 0, tail, head)
        incoming = lax.ppermute(outgoing, "group", [(0, 1), (1, 0)])
        from_low = jnp.where(group_idx == 0, jnp.zeros_like(incoming), incoming)
        from_high = jnp.where(group_idx == 0, incoming, jnp.zeros_like(incoming))
    else:
        forward = [(i, i + 1) for i in range(group_count - 1)]
        backward = [(i + 1, i) for i in range(group_count - 1)]
        from_low = lax.ppermute(tail, "group", forward)
        from_high = lax.ppermute(head, "group", backward)
    low_data, low_params = unpack(from_low, halo, RIM)
    high_data, high_params = unpack(from_high, halo, RIM)
    extended = jnp.concatenate([low_data, row_major, high_data], axis=1)
    params = jnp.concatenate([low_params, table, high_params], axis=0)
    weights = params[:, block_count : 2 * block_count] + (
        params[:, 2 * block_count : 3 * block_count] + params[:, 3 * block_count :]
    )
    params = jnp.concatenate([params[:, :block_count], weights], axis=1)
    bounds = jnp.stack([view_start, total_views]).astype(jnp.int32)
    return rebin_dual(extended, params, bounds, kern_first, kern_second, kern_last)


def solution(mesh):
    return jax.shard_map(
        local,
        mesh=mesh,
        in_specs=(
            P(None, ("group", "dev"), None),
            P(None, ("group", "dev"), None),
            P(),
            P(),
            P(),
            P("group", None),
            P("group", None),
            P(),
            P(),
            P(),
        ),
        out_specs=P("dev", "group", None),
        check_vma=False,
    )
```

```python
import functools

import jax
import jax.numpy as jnp
from jax import lax
from jax.experimental import pallas as pl
from jax.experimental.pallas import tpu as pltpu
from jax.sharding import PartitionSpec as P

REACH = 8
RIM = 2


def conv_kernel(
    table_ref,
    bounds_ref,
    ext_ref,
    w1_ref,
    w2_ref,
    kl_ref,
    out_ref,
    sig_ref,
    feat_ref,
    dual_ref,
    *,
    sig_views,
    block_count,
    col_block,
    channels,
):
    width = block_count * col_block
    first_views = sig_views - 2
    out_views = sig_views - 4
    view_start = bounds_ref[0]
    total_views = bounds_ref[1]
    lane = lax.broadcasted_iota(jnp.int32, (1, width), 1)
    sig_ref[3 * sig_views :, :] = jnp.zeros((sig_ref.shape[0] - 3 * sig_views, width), jnp.float32)
    for u in range(sig_views):
        pos = view_start - RIM + u
        keep = ((pos >= 0) & (pos < total_views)).astype(jnp.float32)
        for k in range(block_count):
            entry = u * 2 * block_count + k
            low = u + table_ref[entry].astype(jnp.int32) + REACH
            frac = table_ref[entry + block_count]
            cols = pl.ds(k * col_block, col_block)
            lower = ext_ref[0, low, :, cols]
            upper = ext_ref[0, low + 1, :, cols]
            value = ((1.0 - frac) * lower + frac * upper).astype(jnp.bfloat16)
            sig_ref[3 * u + 1 : 3 * u + 2, cols] = value.astype(jnp.float32) * keep
        row = sig_ref[3 * u + 1 : 3 * u + 2, :]
        sig_ref[3 * u : 3 * u + 1, :] = jnp.where(lane >= 1, pltpu.roll(row, 1, 1), 0.0)
        sig_ref[3 * u + 2 : 3 * u + 3, :] = jnp.where(
            lane < width - 1, pltpu.roll(row, width - 1, 1), 0.0
        )
    col = lax.broadcasted_iota(jnp.int32, (channels, width), 1)
    keep_left = col >= 1
    keep_right = col < width - 1
    zero = jnp.zeros((channels, width), jnp.bfloat16)
    w1 = w1_ref[...]
    for u in range(first_views):
        taps = sig_ref[3 * u : 3 * u + 16, :].astype(jnp.bfloat16)
        pos = view_start - 1 + u
        scale = ((pos >= 0) & (pos < total_views)).astype(jnp.bfloat16)
        hidden = jnp.dot(w1 * scale, taps, preferred_element_type=jnp.float32)
        hidden = jnp.maximum(hidden, 0.0).astype(jnp.bfloat16)
        base = 3 * u * channels
        feat_ref[base : base + channels, :] = jnp.where(keep_left, pltpu.roll(hidden, 1, 1), zero)
        feat_ref[base + channels : base + 2 * channels, :] = hidden
        feat_ref[base + 2 * channels : base + 3 * channels, :] = jnp.where(
            keep_right, pltpu.roll(hidden, width - 1, 1), zero
        )
    w2 = w2_ref[...]
    kl = kl_ref[...]
    for v in range(out_views):
        window = feat_ref[3 * v * channels : 3 * (v + 3) * channels, :]
        second = jnp.dot(w2, window, preferred_element_type=jnp.float32)
        second = jnp.maximum(second, 0.0).astype(jnp.bfloat16).astype(jnp.float32)
        mix = jnp.sum(kl * second, axis=0, keepdims=True)
        centre = sig_ref[3 * (v + 2) + 1 : 3 * (v + 2) + 2, :]
        dual_ref[v : v + 1, :] = centre + mix
    out_ref[0] = dual_ref[...].astype(out_ref.dtype)


def rebin_dual(extended, table, bounds, kern_first, kern_second, kern_last):
    rows, ext_views, width = extended.shape
    sig_views = table.shape[0]
    block_count = table.shape[1] // 2
    col_block = width // block_count
    channels = kern_first.shape[0]
    first_views = sig_views - 2
    out_views = sig_views - 4
    pad_rows = -(-(3 * first_views + 13) // 8) * 8
    w1 = jnp.pad(kern_first.reshape(channels, 9), ((0, 0), (0, 7)))
    w2 = jnp.transpose(kern_second, (0, 2, 3, 1)).reshape(channels, 9 * channels)
    kl = kern_last.astype(jnp.float32).reshape(channels, 1)
    kernel = functools.partial(
        conv_kernel,
        sig_views=sig_views,
        block_count=block_count,
        col_block=col_block,
        channels=channels,
    )
    grid_spec = pltpu.PrefetchScalarGridSpec(
        num_scalar_prefetch=2,
        grid=(rows,),
        in_specs=[
            pl.BlockSpec((1, ext_views, 1, width), lambda r, *_: (r, 0, 0, 0)),
            pl.BlockSpec((channels, 16), lambda r, *_: (0, 0)),
            pl.BlockSpec((channels, 9 * channels), lambda r, *_: (0, 0)),
            pl.BlockSpec((channels, 1), lambda r, *_: (0, 0)),
        ],
        out_specs=pl.BlockSpec((1, out_views, width), lambda r, *_: (r, 0, 0)),
        scratch_shapes=[
            pltpu.VMEM((pad_rows, width), jnp.float32),
            pltpu.VMEM((first_views * 3 * channels, width), jnp.bfloat16),
            pltpu.VMEM((out_views, width), jnp.float32),
        ],
    )
    return pl.pallas_call(
        kernel,
        out_shape=jax.ShapeDtypeStruct((rows, out_views, width), jnp.bfloat16),
        grid_spec=grid_spec,
    )(
        table.reshape(-1),
        bounds,
        extended.astype(jnp.float32).reshape(rows, ext_views, 1, width),
        w1.astype(jnp.bfloat16),
        w2.astype(jnp.bfloat16),
        kl,
    )


def prepare(mantissa, exponent, poly_square, poly_cube):
    lead_rows, lead_views, width_all = mantissa.shape
    block_count = exponent.shape[2]
    counts = mantissa.astype(jnp.float32).reshape(
        lead_rows, lead_views, block_count, width_all // block_count
    )
    counts = counts * jnp.exp2(-exponent.astype(jnp.float32))[..., None]
    line_int = -jnp.log(counts).reshape(lead_rows, lead_views, width_all)
    hardened = (
        line_int + poly_square * line_int * line_int + poly_cube * line_int * line_int * line_int
    )
    return hardened.astype(jnp.bfloat16)


def resample(hardened, col_map):
    shape_in = hardened.shape
    flat = hardened.reshape(-1, shape_in[2])
    product = jnp.dot(flat, col_map, preferred_element_type=jnp.float32)
    return product.astype(jnp.bfloat16).reshape(shape_in)


def local(
    mantissa,
    exponent,
    poly_square,
    poly_cube,
    col_map,
    rebin_offset,
    rebin_weight,
    kern_first,
    kern_second,
    kern_last,
):
    projected = resample(prepare(mantissa, exponent, poly_square, poly_cube), col_map)
    lead_rows, _, width = projected.shape
    group_count = lax.axis_size("group")
    dev_count = lax.axis_size("dev")
    row_count = lead_rows // dev_count
    block_count = rebin_offset.shape[1]
    view_count = rebin_offset.shape[0]
    total_views = view_count * group_count
    view_start = lax.axis_index("group") * view_count

    weight_high = lax.reduce_precision(rebin_weight, exponent_bits=8, mantissa_bits=7)
    rest = rebin_weight - weight_high
    weight_mid = lax.reduce_precision(rest, exponent_bits=8, mantissa_bits=7)
    weight_low = rest - weight_mid
    table = jnp.concatenate(
        [rebin_offset.astype(jnp.float32), weight_high, weight_mid, weight_low], axis=1
    )
    halo = REACH + RIM
    lead_views = projected.shape[1]
    by_dest = projected.reshape(dev_count, row_count, lead_views, width)
    by_source = lax.all_to_all(by_dest, "dev", 0, 0, tiled=True)
    row_major = jnp.transpose(by_source, (1, 0, 2, 3)).reshape(
        row_count, dev_count * lead_views, width
    )

    def pack(data, params):
        flat = data.reshape(row_count * data.shape[1], width)
        params = params.reshape(-1)
        param_rows = -(-params.shape[0] // width)
        params = jnp.pad(params, (0, param_rows * width - params.shape[0]))
        params = params.astype(jnp.bfloat16).reshape(param_rows, width)
        return jnp.concatenate([flat, params], axis=0)

    def unpack(block, views_in, params_in):
        data = block[: row_count * views_in].reshape(row_count, views_in, width)
        params = block[row_count * views_in :].reshape(-1)[: params_in * 4 * block_count]
        return data, params.astype(jnp.float32).reshape(params_in, 4 * block_count)

    head = pack(row_major[:, :halo], table[:RIM])
    tail = pack(row_major[:, view_count - halo :], table[view_count - RIM :])
    group_idx = lax.axis_index("group")
    if group_count == 2:
        outgoing = jnp.where(group_idx == 0, tail, head)
        incoming = lax.ppermute(outgoing, "group", [(0, 1), (1, 0)])
        from_low = jnp.where(group_idx == 0, jnp.zeros_like(incoming), incoming)
        from_high = jnp.where(group_idx == 0, incoming, jnp.zeros_like(incoming))
    else:
        forward = [(i, i + 1) for i in range(group_count - 1)]
        backward = [(i + 1, i) for i in range(group_count - 1)]
        from_low = lax.ppermute(tail, "group", forward)
        from_high = lax.ppermute(head, "group", backward)
    low_data, low_params = unpack(from_low, halo, RIM)
    high_data, high_params = unpack(from_high, halo, RIM)
    extended = jnp.concatenate([low_data, row_major, high_data], axis=1)
    params = jnp.concatenate([low_params, table, high_params], axis=0)
    weights = params[:, block_count : 2 * block_count] + (
        params[:, 2 * block_count : 3 * block_count] + params[:, 3 * block_count :]
    )
    params = jnp.concatenate([params[:, :block_count], weights], axis=1)
    bounds = jnp.stack([view_start, total_views]).astype(jnp.int32)
    return rebin_dual(extended, params, bounds, kern_first, kern_second, kern_last)


def solution(mesh):
    return jax.shard_map(
        local,
        mesh=mesh,
        in_specs=(
            P(None, ("group", "dev"), None),
            P(None, ("group", "dev"), None),
            P(),
            P(),
            P(),
            P("group", None),
            P("group", None),
            P(),
            P(),
            P(),
        ),
        out_specs=P("dev", "group", None),
        check_vma=False,
    )
```

```python
import functools

import jax
import jax.numpy as jnp
from jax import lax
from jax.experimental import pallas as pl
from jax.experimental.pallas import tpu as pltpu
from jax.sharding import PartitionSpec as P

REACH = 8
RIM = 2


def conv_kernel(
    table_ref,
    bounds_ref,
    ext_ref,
    w1_ref,
    w2_ref,
    kl_ref,
    out_ref,
    sig_ref,
    feat_ref,
    dual_ref,
    *,
    sig_views,
    block_count,
    col_block,
    channels,
):
    width = block_count * col_block
    first_views = sig_views - 2
    out_views = sig_views - 4
    view_start = bounds_ref[0]
    total_views = bounds_ref[1]
    lane = lax.broadcasted_iota(jnp.int32, (1, width), 1)
    sig_ref[3 * sig_views :, :] = jnp.zeros((sig_ref.shape[0] - 3 * sig_views, width), jnp.float32)
    for u in range(sig_views):
        pos = view_start - RIM + u
        keep = ((pos >= 0) & (pos < total_views)).astype(jnp.float32)
        for k in range(block_count):
            entry = u * 2 * block_count + k
            low = u + table_ref[entry].astype(jnp.int32) + REACH
            frac = table_ref[entry + block_count]
            cols = pl.ds(k * col_block, col_block)
            lower = ext_ref[0, low, :, cols]
            upper = ext_ref[0, low + 1, :, cols]
            value = ((1.0 - frac) * lower + frac * upper).astype(jnp.bfloat16)
            sig_ref[3 * u + 1 : 3 * u + 2, cols] = value.astype(jnp.float32) * keep
        row = sig_ref[3 * u + 1 : 3 * u + 2, :]
        sig_ref[3 * u : 3 * u + 1, :] = jnp.where(lane >= 1, pltpu.roll(row, 1, 1), 0.0)
        sig_ref[3 * u + 2 : 3 * u + 3, :] = jnp.where(
            lane < width - 1, pltpu.roll(row, width - 1, 1), 0.0
        )
    col = lax.broadcasted_iota(jnp.int32, (channels, width), 1)
    keep_left = col >= 1
    keep_right = col < width - 1
    w1 = w1_ref[...]
    for u in range(first_views):
        taps = sig_ref[3 * u : 3 * u + 16, :].astype(jnp.bfloat16)
        pos = view_start - 1 + u
        scale = ((pos >= 0) & (pos < total_views)).astype(jnp.bfloat16)
        hidden = jnp.dot(w1 * scale, taps, preferred_element_type=jnp.float32)
        hidden = jnp.maximum(hidden, 0.0).astype(jnp.bfloat16)
        feat_ref[u * channels : (u + 1) * channels, :] = hidden
    w2 = w2_ref[...]
    kl = kl_ref[...]
    for v in range(out_views):
        window = feat_ref[v * channels : (v + 3) * channels, :]
        part = jnp.dot(w2, window, preferred_element_type=jnp.float32)
        second = part[channels : 2 * channels]
        second = second + jnp.where(keep_left, pltpu.roll(part[:channels], 1, 1), 0.0)
        second = second + jnp.where(
            keep_right, pltpu.roll(part[2 * channels :], width - 1, 1), 0.0
        )
        second = jnp.maximum(second, 0.0).astype(jnp.bfloat16).astype(jnp.float32)
        mix = jnp.sum(kl * second, axis=0, keepdims=True)
        centre = sig_ref[3 * (v + 2) + 1 : 3 * (v + 2) + 2, :]
        dual_ref[v : v + 1, :] = centre + mix
    out_ref[0] = dual_ref[...].astype(out_ref.dtype)


def rebin_dual(extended, table, bounds, kern_first, kern_second, kern_last):
    rows, ext_views, width = extended.shape
    sig_views = table.shape[0]
    block_count = table.shape[1] // 2
    col_block = width // block_count
    channels = kern_first.shape[0]
    first_views = sig_views - 2
    out_views = sig_views - 4
    pad_rows = -(-(3 * first_views + 13) // 8) * 8
    w1 = jnp.pad(kern_first.reshape(channels, 9), ((0, 0), (0, 7)))
    w2 = jnp.transpose(kern_second, (3, 0, 2, 1)).reshape(3 * channels, 3 * channels)
    kl = kern_last.astype(jnp.float32).reshape(channels, 1)
    kernel = functools.partial(
        conv_kernel,
        sig_views=sig_views,
        block_count=block_count,
        col_block=col_block,
        channels=channels,
    )
    grid_spec = pltpu.PrefetchScalarGridSpec(
        num_scalar_prefetch=2,
        grid=(rows,),
        in_specs=[
            pl.BlockSpec((1, ext_views, 1, width), lambda r, *_: (r, 0, 0, 0)),
            pl.BlockSpec((channels, 16), lambda r, *_: (0, 0)),
            pl.BlockSpec((3 * channels, 3 * channels), lambda r, *_: (0, 0)),
            pl.BlockSpec((channels, 1), lambda r, *_: (0, 0)),
        ],
        out_specs=pl.BlockSpec((1, out_views, width), lambda r, *_: (r, 0, 0)),
        scratch_shapes=[
            pltpu.VMEM((pad_rows, width), jnp.float32),
            pltpu.VMEM((first_views * channels, width), jnp.bfloat16),
            pltpu.VMEM((out_views, width), jnp.float32),
        ],
    )
    return pl.pallas_call(
        kernel,
        out_shape=jax.ShapeDtypeStruct((rows, out_views, width), jnp.bfloat16),
        grid_spec=grid_spec,
    )(
        table.reshape(-1),
        bounds,
        extended.astype(jnp.float32).reshape(rows, ext_views, 1, width),
        w1.astype(jnp.bfloat16),
        w2.astype(jnp.bfloat16),
        kl,
    )


def prepare(mantissa, exponent, poly_square, poly_cube):
    lead_rows, lead_views, width_all = mantissa.shape
    block_count = exponent.shape[2]
    counts = mantissa.astype(jnp.float32).reshape(
        lead_rows, lead_views, block_count, width_all // block_count
    )
    counts = counts * jnp.exp2(-exponent.astype(jnp.float32))[..., None]
    line_int = -jnp.log(counts).reshape(lead_rows, lead_views, width_all)
    hardened = (
        line_int + poly_square * line_int * line_int + poly_cube * line_int * line_int * line_int
    )
    return hardened.astype(jnp.bfloat16)


def resample(hardened, col_map):
    shape_in = hardened.shape
    flat = hardened.reshape(-1, shape_in[2])
    product = jnp.dot(flat, col_map, preferred_element_type=jnp.float32)
    return product.astype(jnp.bfloat16).reshape(shape_in)


def local(
    mantissa,
    exponent,
    poly_square,
    poly_cube,
    col_map,
    rebin_offset,
    rebin_weight,
    kern_first,
    kern_second,
    kern_last,
):
    projected = resample(prepare(mantissa, exponent, poly_square, poly_cube), col_map)
    lead_rows, _, width = projected.shape
    group_count = lax.axis_size("group")
    dev_count = lax.axis_size("dev")
    row_count = lead_rows // dev_count
    block_count = rebin_offset.shape[1]
    view_count = rebin_offset.shape[0]
    total_views = view_count * group_count
    view_start = lax.axis_index("group") * view_count

    weight_high = lax.reduce_precision(rebin_weight, exponent_bits=8, mantissa_bits=7)
    rest = rebin_weight - weight_high
    weight_mid = lax.reduce_precision(rest, exponent_bits=8, mantissa_bits=7)
    weight_low = rest - weight_mid
    table = jnp.concatenate(
        [rebin_offset.astype(jnp.float32), weight_high, weight_mid, weight_low], axis=1
    )
    halo = REACH + RIM
    lead_views = projected.shape[1]
    by_dest = projected.reshape(dev_count, row_count, lead_views, width)
    by_source = lax.all_to_all(by_dest, "dev", 0, 0, tiled=True)
    row_major = jnp.transpose(by_source, (1, 0, 2, 3)).reshape(
        row_count, dev_count * lead_views, width
    )

    def pack(data, params):
        flat = data.reshape(row_count * data.shape[1], width)
        params = params.reshape(-1)
        param_rows = -(-params.shape[0] // width)
        params = jnp.pad(params, (0, param_rows * width - params.shape[0]))
        params = params.astype(jnp.bfloat16).reshape(param_rows, width)
        return jnp.concatenate([flat, params], axis=0)

    def unpack(block, views_in, params_in):
        data = block[: row_count * views_in].reshape(row_count, views_in, width)
        params = block[row_count * views_in :].reshape(-1)[: params_in * 4 * block_count]
        return data, params.astype(jnp.float32).reshape(params_in, 4 * block_count)

    head = pack(row_major[:, :halo], table[:RIM])
    tail = pack(row_major[:, view_count - halo :], table[view_count - RIM :])
    group_idx = lax.axis_index("group")
    if group_count == 2:
        outgoing = jnp.where(group_idx == 0, tail, head)
        incoming = lax.ppermute(outgoing, "group", [(0, 1), (1, 0)])
        from_low = jnp.where(group_idx == 0, jnp.zeros_like(incoming), incoming)
        from_high = jnp.where(group_idx == 0, incoming, jnp.zeros_like(incoming))
    else:
        forward = [(i, i + 1) for i in range(group_count - 1)]
        backward = [(i + 1, i) for i in range(group_count - 1)]
        from_low = lax.ppermute(tail, "group", forward)
        from_high = lax.ppermute(head, "group", backward)
    low_data, low_params = unpack(from_low, halo, RIM)
    high_data, high_params = unpack(from_high, halo, RIM)
    extended = jnp.concatenate([low_data, row_major, high_data], axis=1)
    params = jnp.concatenate([low_params, table, high_params], axis=0)
    weights = params[:, block_count : 2 * block_count] + (
        params[:, 2 * block_count : 3 * block_count] + params[:, 3 * block_count :]
    )
    params = jnp.concatenate([params[:, :block_count], weights], axis=1)
    bounds = jnp.stack([view_start, total_views]).astype(jnp.int32)
    return rebin_dual(extended, params, bounds, kern_first, kern_second, kern_last)


def solution(mesh):
    return jax.shard_map(
        local,
        mesh=mesh,
        in_specs=(
            P(None, ("group", "dev"), None),
            P(None, ("group", "dev"), None),
            P(),
            P(),
            P(),
            P("group", None),
            P("group", None),
            P(),
            P(),
            P(),
        ),
        out_specs=P("dev", "group", None),
        check_vma=False,
    )
```

```python
import functools

import jax
import jax.numpy as jnp
from jax import lax
from jax.experimental import pallas as pl
from jax.experimental.pallas import tpu as pltpu
from jax.sharding import PartitionSpec as P

REACH = 8
RIM = 2


def conv_kernel(
    table_ref,
    bounds_ref,
    ext_ref,
    w1_ref,
    w2_ref,
    kl_ref,
    out_ref,
    sig_ref,
    feat_ref,
    dual_ref,
    *,
    sig_views,
    block_count,
    col_block,
    channels,
):
    width = block_count * col_block
    first_views = sig_views - 2
    out_views = sig_views - 4
    view_start = bounds_ref[0]
    total_views = bounds_ref[1]
    lane = lax.broadcasted_iota(jnp.int32, (1, width), 1)
    sig_ref[3 * sig_views :, :] = jnp.zeros((sig_ref.shape[0] - 3 * sig_views, width), jnp.float32)
    for u in range(sig_views):
        pos = view_start - RIM + u
        keep = ((pos >= 0) & (pos < total_views)).astype(jnp.float32)
        for k in range(block_count):
            entry = u * 2 * block_count + k
            low = u + table_ref[entry].astype(jnp.int32) + REACH
            frac = table_ref[entry + block_count]
            cols = pl.ds(k * col_block, col_block)
            lower = ext_ref[0, low, :, cols]
            upper = ext_ref[0, low + 1, :, cols]
            value = ((1.0 - frac) * lower + frac * upper).astype(jnp.bfloat16)
            sig_ref[3 * u + 1 : 3 * u + 2, cols] = value.astype(jnp.float32) * keep
        row = sig_ref[3 * u + 1 : 3 * u + 2, :]
        sig_ref[3 * u : 3 * u + 1, :] = jnp.where(lane >= 1, pltpu.roll(row, 1, 1), 0.0)
        sig_ref[3 * u + 2 : 3 * u + 3, :] = jnp.where(
            lane < width - 1, pltpu.roll(row, width - 1, 1), 0.0
        )
    col = lax.broadcasted_iota(jnp.int32, (channels, width), 1)
    keep_left = col >= 1
    keep_right = col < width - 1
    w1 = w1_ref[...]
    for u in range(first_views):
        taps = sig_ref[3 * u : 3 * u + 16, :].astype(jnp.bfloat16)
        pos = view_start - 1 + u
        scale = ((pos >= 0) & (pos < total_views)).astype(jnp.bfloat16)
        hidden = jnp.dot(w1 * scale, taps, preferred_element_type=jnp.float32)
        hidden = jnp.maximum(hidden, 0.0).astype(jnp.bfloat16)
        feat_ref[u * channels : (u + 1) * channels, :] = hidden
    w2 = w2_ref[...]
    kl = kl_ref[...]
    for v in range(out_views):
        window = feat_ref[v * channels : (v + 3) * channels, :]
        part = jnp.dot(w2, window, preferred_element_type=jnp.float32)
        second = part[channels : 2 * channels]
        second = second + jnp.where(keep_left, pltpu.roll(part[:channels], 1, 1), 0.0)
        second = second + jnp.where(
            keep_right, pltpu.roll(part[2 * channels :], width - 1, 1), 0.0
        )
        second = jnp.maximum(second, 0.0).astype(jnp.bfloat16).astype(jnp.float32)
        mix = jnp.sum(kl * second, axis=0, keepdims=True)
        centre = sig_ref[3 * (v + 2) + 1 : 3 * (v + 2) + 2, :]
        dual_ref[v : v + 1, :] = centre + mix
    out_ref[0] = dual_ref[...].astype(out_ref.dtype)


def rebin_dual(extended, table, bounds, kern_first, kern_second, kern_last):
    rows, ext_views, width = extended.shape
    sig_views = table.shape[0]
    block_count = table.shape[1] // 2
    col_block = width // block_count
    channels = kern_first.shape[0]
    first_views = sig_views - 2
    out_views = sig_views - 4
    pad_rows = -(-(3 * first_views + 13) // 8) * 8
    w1 = jnp.pad(kern_first.reshape(channels, 9), ((0, 0), (0, 7)))
    w2 = jnp.transpose(kern_second, (3, 0, 2, 1)).reshape(3 * channels, 3 * channels)
    kl = kern_last.astype(jnp.float32).reshape(channels, 1)
    kernel = functools.partial(
        conv_kernel,
        sig_views=sig_views,
        block_count=block_count,
        col_block=col_block,
        channels=channels,
    )
    grid_spec = pltpu.PrefetchScalarGridSpec(
        num_scalar_prefetch=2,
        grid=(rows,),
        in_specs=[
            pl.BlockSpec((1, ext_views, 1, width), lambda r, *_: (r, 0, 0, 0)),
            pl.BlockSpec((channels, 16), lambda r, *_: (0, 0)),
            pl.BlockSpec((3 * channels, 3 * channels), lambda r, *_: (0, 0)),
            pl.BlockSpec((channels, 1), lambda r, *_: (0, 0)),
        ],
        out_specs=pl.BlockSpec((1, out_views, width), lambda r, *_: (r, 0, 0)),
        scratch_shapes=[
            pltpu.VMEM((pad_rows, width), jnp.float32),
            pltpu.VMEM((first_views * channels, width), jnp.bfloat16),
            pltpu.VMEM((out_views, width), jnp.float32),
        ],
    )
    return pl.pallas_call(
        kernel,
        out_shape=jax.ShapeDtypeStruct((rows, out_views, width), jnp.bfloat16),
        grid_spec=grid_spec,
    )(
        table.reshape(-1),
        bounds,
        extended.astype(jnp.float32).reshape(rows, ext_views, 1, width),
        w1.astype(jnp.bfloat16),
        w2.astype(jnp.bfloat16),
        kl,
    )


def prepare(mantissa, exponent, poly_square, poly_cube):
    lead_rows, lead_views, width_all = mantissa.shape
    block_count = exponent.shape[2]
    counts = mantissa.astype(jnp.float32).reshape(
        lead_rows, lead_views, block_count, width_all // block_count
    )
    counts = counts * jnp.exp2(-exponent.astype(jnp.float32))[..., None]
    line_int = -jnp.log(counts).reshape(lead_rows, lead_views, width_all)
    hardened = (
        line_int + poly_square * line_int * line_int + poly_cube * line_int * line_int * line_int
    )
    return hardened.astype(jnp.bfloat16)


def resample(hardened, col_map):
    shape_in = hardened.shape
    flat = hardened.reshape(-1, shape_in[2])
    product = jnp.dot(flat, col_map, preferred_element_type=jnp.float32)
    return product.astype(jnp.bfloat16).reshape(shape_in)


def local(
    mantissa,
    exponent,
    poly_square,
    poly_cube,
    col_map,
    rebin_offset,
    rebin_weight,
    kern_first,
    kern_second,
    kern_last,
):
    projected = resample(prepare(mantissa, exponent, poly_square, poly_cube), col_map)
    lead_rows, _, width = projected.shape
    group_count = lax.axis_size("group")
    dev_count = lax.axis_size("dev")
    row_count = lead_rows // dev_count
    block_count = rebin_offset.shape[1]
    view_count = rebin_offset.shape[0]
    total_views = view_count * group_count
    view_start = lax.axis_index("group") * view_count

    weight_high = lax.reduce_precision(rebin_weight, exponent_bits=8, mantissa_bits=7)
    rest = rebin_weight - weight_high
    weight_mid = lax.reduce_precision(rest, exponent_bits=8, mantissa_bits=7)
    weight_low = rest - weight_mid
    table = jnp.concatenate(
        [rebin_offset.astype(jnp.float32), weight_high, weight_mid, weight_low], axis=1
    )
    halo = REACH + RIM
    lead_views = projected.shape[1]
    by_dest = projected.reshape(dev_count, row_count, lead_views, width)
    by_source = lax.all_to_all(by_dest, "dev", 0, 0, tiled=True)
    row_major = jnp.transpose(by_source, (1, 0, 2, 3)).reshape(
        row_count, dev_count * lead_views, width
    )

    def pack(data, params):
        flat = data.reshape(row_count * data.shape[1], width)
        params = params.reshape(-1)
        param_rows = -(-params.shape[0] // width)
        params = jnp.pad(params, (0, param_rows * width - params.shape[0]))
        params = params.astype(jnp.bfloat16).reshape(param_rows, width)
        return jnp.concatenate([flat, params], axis=0)

    def unpack(block, views_in, params_in):
        data = block[: row_count * views_in].reshape(row_count, views_in, width)
        params = block[row_count * views_in :].reshape(-1)[: params_in * 4 * block_count]
        return data, params.astype(jnp.float32).reshape(params_in, 4 * block_count)

    head = pack(row_major[:, :halo], table[:RIM])
    tail = pack(row_major[:, view_count - halo :], table[view_count - RIM :])
    group_idx = lax.axis_index("group")
    if group_count == 2:
        outgoing = jnp.where(group_idx == 0, tail, head)
        incoming = lax.ppermute(outgoing, "group", [(0, 1), (1, 0)])
        from_low = jnp.where(group_idx == 0, jnp.zeros_like(incoming), incoming)
        from_high = jnp.where(group_idx == 0, incoming, jnp.zeros_like(incoming))
    else:
        forward = [(i, i + 1) for i in range(group_count - 1)]
        backward = [(i + 1, i) for i in range(group_count - 1)]
        from_low = lax.ppermute(tail, "group", forward)
        from_high = lax.ppermute(head, "group", backward)
    low_data, low_params = unpack(from_low, halo, RIM)
    high_data, high_params = unpack(from_high, halo, RIM)
    extended = jnp.concatenate([low_data, row_major, high_data], axis=1)
    params = jnp.concatenate([low_params, table, high_params], axis=0)
    weights = params[:, block_count : 2 * block_count] + (
        params[:, 2 * block_count : 3 * block_count] + params[:, 3 * block_count :]
    )
    params = jnp.concatenate([params[:, :block_count], weights], axis=1)
    bounds = jnp.stack([view_start, total_views]).astype(jnp.int32)
    return rebin_dual(extended, params, bounds, kern_first, kern_second, kern_last)


def local_swapped(
    mantissa,
    exponent,
    poly_square,
    poly_cube,
    col_map,
    rebin_offset,
    rebin_weight,
    kern_first,
    kern_second,
    kern_last,
):
    lead_rows, lead_views, width = mantissa.shape
    dev_count = lax.axis_size("dev")
    row_count = lead_rows // dev_count
    view_count, block_count = rebin_offset.shape
    total_views = 2 * view_count
    first_group = lax.axis_index("group") == 0
    view_start = jnp.where(first_group, 0, view_count)

    weight_high = lax.reduce_precision(rebin_weight, exponent_bits=8, mantissa_bits=7)
    rest = rebin_weight - weight_high
    weight_mid = lax.reduce_precision(rest, exponent_bits=8, mantissa_bits=7)
    weight_low = rest - weight_mid
    table = jnp.concatenate(
        [rebin_offset.astype(jnp.float32), weight_high, weight_mid, weight_low], axis=1
    )

    def as_rows(values):
        values = values.reshape(-1)
        count = -(-values.shape[0] // width)
        values = jnp.pad(values, (0, count * width - values.shape[0]))
        return values.astype(jnp.bfloat16).reshape(count, width)

    data_rows = lead_rows * lead_views
    exp_rows = as_rows(exponent.astype(jnp.float32))
    packet = jnp.concatenate(
        [mantissa.reshape(data_rows, width), exp_rows, as_rows(table)], axis=0
    )
    arrived = lax.ppermute(packet, "group", [(0, 1), (1, 0)])
    other_mantissa = arrived[:data_rows].reshape(lead_rows, lead_views, width)
    exp_size = exponent.size
    other_exponent = arrived[data_rows : data_rows + exp_rows.shape[0]].reshape(-1)[:exp_size]
    other_exponent = other_exponent.astype(jnp.int32).reshape(exponent.shape)
    other_table = arrived[data_rows + exp_rows.shape[0] :].reshape(-1)[: table.size]
    other_table = other_table.astype(jnp.float32).reshape(table.shape)
    both_mantissa = jnp.concatenate([mantissa, other_mantissa], axis=1)
    both_exponent = jnp.concatenate([exponent, other_exponent], axis=1)
    projected = resample(prepare(both_mantissa, both_exponent, poly_square, poly_cube), col_map)

    by_dest = projected.reshape(dev_count, row_count, 2, lead_views, width)
    by_source = lax.all_to_all(by_dest, "dev", 0, 0, tiled=True)
    slots = jnp.transpose(by_source, (1, 2, 0, 3, 4)).reshape(
        row_count, 2, view_count, width
    )
    own_views, other_views = slots[:, 0], slots[:, 1]
    all_views = jnp.where(
        first_group,
        jnp.concatenate([own_views, other_views], axis=1),
        jnp.concatenate([other_views, own_views], axis=1),
    )
    halo = REACH + RIM
    all_views = jnp.pad(all_views, ((0, 0), (halo, halo), (0, 0)))
    extended = lax.dynamic_slice_in_dim(all_views, view_start, view_count + 2 * halo, axis=1)
    full_table = jnp.where(
        first_group,
        jnp.concatenate([table, other_table], axis=0),
        jnp.concatenate([other_table, table], axis=0),
    )
    full_table = jnp.pad(full_table, ((RIM, RIM), (0, 0)))
    params = lax.dynamic_slice_in_dim(full_table, view_start, view_count + 2 * RIM, axis=0)
    weights = params[:, block_count : 2 * block_count] + (
        params[:, 2 * block_count : 3 * block_count] + params[:, 3 * block_count :]
    )
    params = jnp.concatenate([params[:, :block_count], weights], axis=1)
    bounds = jnp.stack([view_start, total_views]).astype(jnp.int32)
    return rebin_dual(extended, params, bounds, kern_first, kern_second, kern_last)


def solution(mesh):
    body = local_swapped if mesh.shape["group"] == 2 else local
    return jax.shard_map(
        body,
        mesh=mesh,
        in_specs=(
            P(None, ("group", "dev"), None),
            P(None, ("group", "dev"), None),
            P(),
            P(),
            P(),
            P("group", None),
            P("group", None),
            P(),
            P(),
            P(),
        ),
        out_specs=P("dev", "group", None),
        check_vma=False,
    )
```

```python
import functools

import jax
import jax.numpy as jnp
from jax import lax
from jax.experimental import pallas as pl
from jax.experimental.pallas import tpu as pltpu
from jax.sharding import PartitionSpec as P

REACH = 8
RIM = 2


def conv_kernel(
    table_ref,
    bounds_ref,
    ext_ref,
    w1_ref,
    w2_ref,
    kl_ref,
    out_ref,
    sig_ref,
    feat_ref,
    dual_ref,
    *,
    sig_views,
    block_count,
    col_block,
    channels,
):
    width = block_count * col_block
    first_views = sig_views - 2
    out_views = sig_views - 4
    view_start = bounds_ref[0]
    total_views = bounds_ref[1]
    lane = lax.broadcasted_iota(jnp.int32, (1, width), 1)
    sig_ref[3 * sig_views :, :] = jnp.zeros((sig_ref.shape[0] - 3 * sig_views, width), jnp.float32)
    for u in range(sig_views):
        pos = view_start - RIM + u
        keep = ((pos >= 0) & (pos < total_views)).astype(jnp.float32)
        for k in range(block_count):
            entry = u * 2 * block_count + k
            low = u + table_ref[entry].astype(jnp.int32) + REACH
            frac = table_ref[entry + block_count]
            cols = pl.ds(k * col_block, col_block)
            lower = ext_ref[0, low, :, cols]
            upper = ext_ref[0, low + 1, :, cols]
            value = ((1.0 - frac) * lower + frac * upper).astype(jnp.bfloat16)
            sig_ref[3 * u + 1 : 3 * u + 2, cols] = value.astype(jnp.float32) * keep
        row = sig_ref[3 * u + 1 : 3 * u + 2, :]
        sig_ref[3 * u : 3 * u + 1, :] = jnp.where(lane >= 1, pltpu.roll(row, 1, 1), 0.0)
        sig_ref[3 * u + 2 : 3 * u + 3, :] = jnp.where(
            lane < width - 1, pltpu.roll(row, width - 1, 1), 0.0
        )
    col = lax.broadcasted_iota(jnp.int32, (channels, width), 1)
    keep_left = col >= 1
    keep_right = col < width - 1
    w1 = w1_ref[...]
    for u in range(first_views):
        taps = sig_ref[3 * u : 3 * u + 16, :].astype(jnp.bfloat16)
        pos = view_start - 1 + u
        scale = ((pos >= 0) & (pos < total_views)).astype(jnp.bfloat16)
        hidden = jnp.dot(w1 * scale, taps, preferred_element_type=jnp.float32)
        hidden = jnp.maximum(hidden, 0.0).astype(jnp.bfloat16)
        feat_ref[u * channels : (u + 1) * channels, :] = hidden
    w2 = w2_ref[...]
    kl = kl_ref[...]
    for v in range(out_views):
        window = feat_ref[v * channels : (v + 3) * channels, :]
        part = jnp.dot(w2, window, preferred_element_type=jnp.float32)
        second = part[channels : 2 * channels]
        second = second + jnp.where(keep_left, pltpu.roll(part[:channels], 1, 1), 0.0)
        second = second + jnp.where(
            keep_right, pltpu.roll(part[2 * channels :], width - 1, 1), 0.0
        )
        second = jnp.maximum(second, 0.0).astype(jnp.bfloat16).astype(jnp.float32)
        mix = jnp.sum(kl * second, axis=0, keepdims=True)
        centre = sig_ref[3 * (v + 2) + 1 : 3 * (v + 2) + 2, :]
        dual_ref[v : v + 1, :] = centre + mix
    out_ref[0] = dual_ref[...].astype(out_ref.dtype)


def rebin_dual(extended, table, bounds, kern_first, kern_second, kern_last):
    rows, ext_views, width = extended.shape
    sig_views = table.shape[0]
    block_count = table.shape[1] // 2
    col_block = width // block_count
    channels = kern_first.shape[0]
    first_views = sig_views - 2
    out_views = sig_views - 4
    pad_rows = -(-(3 * first_views + 13) // 8) * 8
    w1 = jnp.pad(kern_first.reshape(channels, 9), ((0, 0), (0, 7)))
    w2 = jnp.transpose(kern_second, (3, 0, 2, 1)).reshape(3 * channels, 3 * channels)
    kl = kern_last.astype(jnp.float32).reshape(channels, 1)
    kernel = functools.partial(
        conv_kernel,
        sig_views=sig_views,
        block_count=block_count,
        col_block=col_block,
        channels=channels,
    )
    grid_spec = pltpu.PrefetchScalarGridSpec(
        num_scalar_prefetch=2,
        grid=(rows,),
        in_specs=[
            pl.BlockSpec((1, ext_views, 1, width), lambda r, *_: (r, 0, 0, 0)),
            pl.BlockSpec((channels, 16), lambda r, *_: (0, 0)),
            pl.BlockSpec((3 * channels, 3 * channels), lambda r, *_: (0, 0)),
            pl.BlockSpec((channels, 1), lambda r, *_: (0, 0)),
        ],
        out_specs=pl.BlockSpec((1, out_views, width), lambda r, *_: (r, 0, 0)),
        scratch_shapes=[
            pltpu.VMEM((pad_rows, width), jnp.float32),
            pltpu.VMEM((first_views * channels, width), jnp.bfloat16),
            pltpu.VMEM((out_views, width), jnp.float32),
        ],
    )
    return pl.pallas_call(
        kernel,
        out_shape=jax.ShapeDtypeStruct((rows, out_views, width), jnp.bfloat16),
        grid_spec=grid_spec,
    )(
        table.reshape(-1),
        bounds,
        extended.astype(jnp.float32).reshape(rows, ext_views, 1, width),
        w1.astype(jnp.bfloat16),
        w2.astype(jnp.bfloat16),
        kl,
    )


def prepare(mantissa, exponent, poly_square, poly_cube):
    lead_rows, lead_views, width_all = mantissa.shape
    block_count = exponent.shape[2]
    counts = mantissa.astype(jnp.float32).reshape(
        lead_rows, lead_views, block_count, width_all // block_count
    )
    counts = counts * jnp.exp2(-exponent.astype(jnp.float32))[..., None]
    line_int = -jnp.log(counts).reshape(lead_rows, lead_views, width_all)
    hardened = (
        line_int + poly_square * line_int * line_int + poly_cube * line_int * line_int * line_int
    )
    return hardened.astype(jnp.bfloat16)


def resample(hardened, col_map):
    shape_in = hardened.shape
    flat = hardened.reshape(-1, shape_in[2])
    product = jnp.dot(flat, col_map, preferred_element_type=jnp.float32)
    return product.astype(jnp.bfloat16).reshape(shape_in)


def local(
    mantissa,
    exponent,
    poly_square,
    poly_cube,
    col_map,
    rebin_offset,
    rebin_weight,
    kern_first,
    kern_second,
    kern_last,
):
    projected = resample(prepare(mantissa, exponent, poly_square, poly_cube), col_map)
    lead_rows, _, width = projected.shape
    group_count = lax.axis_size("group")
    dev_count = lax.axis_size("dev")
    row_count = lead_rows // dev_count
    block_count = rebin_offset.shape[1]
    view_count = rebin_offset.shape[0]
    total_views = view_count * group_count
    view_start = lax.axis_index("group") * view_count

    weight_high = lax.reduce_precision(rebin_weight, exponent_bits=8, mantissa_bits=7)
    rest = rebin_weight - weight_high
    weight_mid = lax.reduce_precision(rest, exponent_bits=8, mantissa_bits=7)
    weight_low = rest - weight_mid
    table = jnp.concatenate(
        [rebin_offset.astype(jnp.float32), weight_high, weight_mid, weight_low], axis=1
    )
    halo = REACH + RIM
    lead_views = projected.shape[1]
    by_dest = projected.reshape(dev_count, row_count, lead_views, width)
    by_source = lax.all_to_all(by_dest, "dev", 0, 0, tiled=True)
    row_major = jnp.transpose(by_source, (1, 0, 2, 3)).reshape(
        row_count, dev_count * lead_views, width
    )

    def pack(data, params):
        flat = data.reshape(row_count * data.shape[1], width)
        params = params.reshape(-1)
        param_rows = -(-params.shape[0] // width)
        params = jnp.pad(params, (0, param_rows * width - params.shape[0]))
        params = params.astype(jnp.bfloat16).reshape(param_rows, width)
        return jnp.concatenate([flat, params], axis=0)

    def unpack(block, views_in, params_in):
        data = block[: row_count * views_in].reshape(row_count, views_in, width)
        params = block[row_count * views_in :].reshape(-1)[: params_in * 4 * block_count]
        return data, params.astype(jnp.float32).reshape(params_in, 4 * block_count)

    group_idx = lax.axis_index("group")
    if group_count == 2:
        first = group_idx == 0
        outgoing = pack(
            jnp.where(first, row_major[:, view_count - halo :], row_major[:, :halo]),
            jnp.where(first, table[view_count - RIM :], table[:RIM]),
        )
        incoming = lax.ppermute(outgoing, "group", [(0, 1), (1, 0)])
        other_data, other_params = unpack(incoming, halo, RIM)
        blank_data = jnp.zeros_like(other_data)
        blank_params = jnp.zeros_like(other_params)
        extended = jnp.where(
            first,
            jnp.concatenate([blank_data, row_major, other_data], axis=1),
            jnp.concatenate([other_data, row_major, blank_data], axis=1),
        )
        params = jnp.where(
            first,
            jnp.concatenate([blank_params, table, other_params], axis=0),
            jnp.concatenate([other_params, table, blank_params], axis=0),
        )
    else:
        head = pack(row_major[:, :halo], table[:RIM])
        tail = pack(row_major[:, view_count - halo :], table[view_count - RIM :])
        forward = [(i, i + 1) for i in range(group_count - 1)]
        backward = [(i + 1, i) for i in range(group_count - 1)]
        low_data, low_params = unpack(lax.ppermute(tail, "group", forward), halo, RIM)
        high_data, high_params = unpack(lax.ppermute(head, "group", backward), halo, RIM)
        extended = jnp.concatenate([low_data, row_major, high_data], axis=1)
        params = jnp.concatenate([low_params, table, high_params], axis=0)
    weights = params[:, block_count : 2 * block_count] + (
        params[:, 2 * block_count : 3 * block_count] + params[:, 3 * block_count :]
    )
    params = jnp.concatenate([params[:, :block_count], weights], axis=1)
    bounds = jnp.stack([view_start, total_views]).astype(jnp.int32)
    return rebin_dual(extended, params, bounds, kern_first, kern_second, kern_last)


def solution(mesh):
    return jax.shard_map(
        local,
        mesh=mesh,
        in_specs=(
            P(None, ("group", "dev"), None),
            P(None, ("group", "dev"), None),
            P(),
            P(),
            P(),
            P("group", None),
            P("group", None),
            P(),
            P(),
            P(),
        ),
        out_specs=P("dev", "group", None),
        check_vma=False,
    )
```

```python
import functools

import jax
import jax.numpy as jnp
from jax import lax
from jax.experimental import pallas as pl
from jax.experimental.pallas import tpu as pltpu
from jax.sharding import PartitionSpec as P

REACH = 8
RIM = 2


def conv_kernel(
    table_ref,
    bounds_ref,
    ext_ref,
    w1_ref,
    w2_ref,
    kl_ref,
    out_ref,
    sig_ref,
    feat_ref,
    dual_ref,
    *,
    sig_views,
    block_count,
    col_block,
    channels,
):
    width = block_count * col_block
    first_views = sig_views - 2
    out_views = sig_views - 4
    view_start = bounds_ref[0]
    total_views = bounds_ref[1]
    lane = lax.broadcasted_iota(jnp.int32, (1, width), 1)
    sig_ref[3 * sig_views :, :] = jnp.zeros((sig_ref.shape[0] - 3 * sig_views, width), jnp.float32)
    for u in range(sig_views):
        pos = view_start - RIM + u
        keep = ((pos >= 0) & (pos < total_views)).astype(jnp.float32)
        for k in range(block_count):
            entry = u * 2 * block_count + k
            low = u + table_ref[entry].astype(jnp.int32) + REACH
            frac = table_ref[entry + block_count]
            cols = pl.ds(k * col_block, col_block)
            lower = ext_ref[0, low, :, cols]
            upper = ext_ref[0, low + 1, :, cols]
            value = ((1.0 - frac) * lower + frac * upper).astype(jnp.bfloat16)
            sig_ref[3 * u + 1 : 3 * u + 2, cols] = value.astype(jnp.float32) * keep
        row = sig_ref[3 * u + 1 : 3 * u + 2, :]
        sig_ref[3 * u : 3 * u + 1, :] = jnp.where(lane >= 1, pltpu.roll(row, 1, 1), 0.0)
        sig_ref[3 * u + 2 : 3 * u + 3, :] = jnp.where(
            lane < width - 1, pltpu.roll(row, width - 1, 1), 0.0
        )
    col = lax.broadcasted_iota(jnp.int32, (channels, width), 1)
    keep_left = col >= 1
    keep_right = col < width - 1
    w1 = w1_ref[...]
    for u in range(first_views):
        taps = sig_ref[3 * u : 3 * u + 16, :].astype(jnp.bfloat16)
        pos = view_start - 1 + u
        scale = ((pos >= 0) & (pos < total_views)).astype(jnp.bfloat16)
        hidden = jnp.dot(w1 * scale, taps, preferred_element_type=jnp.float32)
        hidden = jnp.maximum(hidden, 0.0).astype(jnp.bfloat16)
        feat_ref[u * channels : (u + 1) * channels, :] = hidden
    w2 = w2_ref[...]
    kl = kl_ref[...]
    for v in range(out_views):
        window = feat_ref[v * channels : (v + 3) * channels, :]
        part = jnp.dot(w2, window, preferred_element_type=jnp.float32)
        second = part[channels : 2 * channels]
        second = second + jnp.where(keep_left, pltpu.roll(part[:channels], 1, 1), 0.0)
        second = second + jnp.where(
            keep_right, pltpu.roll(part[2 * channels :], width - 1, 1), 0.0
        )
        second = jnp.maximum(second, 0.0).astype(jnp.bfloat16).astype(jnp.float32)
        mix = jnp.sum(kl * second, axis=0, keepdims=True)
        centre = sig_ref[3 * (v + 2) + 1 : 3 * (v + 2) + 2, :]
        dual_ref[v : v + 1, :] = centre + mix
    out_ref[0] = dual_ref[...].astype(out_ref.dtype)


def rebin_dual(extended, table, bounds, kern_first, kern_second, kern_last):
    rows, ext_views, width = extended.shape
    sig_views = table.shape[0]
    block_count = table.shape[1] // 2
    col_block = width // block_count
    channels = kern_first.shape[0]
    first_views = sig_views - 2
    out_views = sig_views - 4
    pad_rows = -(-(3 * first_views + 13) // 8) * 8
    w1 = jnp.pad(kern_first.reshape(channels, 9), ((0, 0), (0, 7)))
    w2 = jnp.transpose(kern_second, (3, 0, 2, 1)).reshape(3 * channels, 3 * channels)
    kl = kern_last.astype(jnp.float32).reshape(channels, 1)
    kernel = functools.partial(
        conv_kernel,
        sig_views=sig_views,
        block_count=block_count,
        col_block=col_block,
        channels=channels,
    )
    grid_spec = pltpu.PrefetchScalarGridSpec(
        num_scalar_prefetch=2,
        grid=(rows,),
        in_specs=[
            pl.BlockSpec((1, ext_views, 1, width), lambda r, *_: (r, 0, 0, 0)),
            pl.BlockSpec((channels, 16), lambda r, *_: (0, 0)),
            pl.BlockSpec((3 * channels, 3 * channels), lambda r, *_: (0, 0)),
            pl.BlockSpec((channels, 1), lambda r, *_: (0, 0)),
        ],
        out_specs=pl.BlockSpec((1, out_views, width), lambda r, *_: (r, 0, 0)),
        scratch_shapes=[
            pltpu.VMEM((pad_rows, width), jnp.float32),
            pltpu.VMEM((first_views * channels, width), jnp.bfloat16),
            pltpu.VMEM((out_views, width), jnp.float32),
        ],
    )
    return pl.pallas_call(
        kernel,
        out_shape=jax.ShapeDtypeStruct((rows, out_views, width), jnp.bfloat16),
        grid_spec=grid_spec,
    )(
        table.reshape(-1),
        bounds,
        extended.astype(jnp.float32).reshape(rows, ext_views, 1, width),
        w1.astype(jnp.bfloat16),
        w2.astype(jnp.bfloat16),
        kl,
    )


def prepare(mantissa, exponent, poly_square, poly_cube):
    lead_rows, lead_views, width_all = mantissa.shape
    block_count = exponent.shape[2]
    counts = mantissa.astype(jnp.float32).reshape(
        lead_rows, lead_views, block_count, width_all // block_count
    )
    counts = counts * jnp.exp2(-exponent.astype(jnp.float32))[..., None]
    line_int = -jnp.log(counts).reshape(lead_rows, lead_views, width_all)
    hardened = (
        line_int + poly_square * line_int * line_int + poly_cube * line_int * line_int * line_int
    )
    return hardened.astype(jnp.bfloat16)


def resample(hardened, col_map):
    shape_in = hardened.shape
    flat = hardened.reshape(-1, shape_in[2])
    product = jnp.dot(flat, col_map, preferred_element_type=jnp.float32)
    return product.astype(jnp.bfloat16).reshape(shape_in)


def local(
    mantissa,
    exponent,
    poly_square,
    poly_cube,
    col_map,
    rebin_offset,
    rebin_weight,
    kern_first,
    kern_second,
    kern_last,
):
    projected = resample(prepare(mantissa, exponent, poly_square, poly_cube), col_map)
    lead_rows, _, width = projected.shape
    group_count = lax.axis_size("group")
    dev_count = lax.axis_size("dev")
    row_count = lead_rows // dev_count
    block_count = rebin_offset.shape[1]
    view_count = rebin_offset.shape[0]
    total_views = view_count * group_count
    view_start = lax.axis_index("group") * view_count

    weight_high = lax.reduce_precision(rebin_weight, exponent_bits=8, mantissa_bits=7)
    rest = rebin_weight - weight_high
    weight_mid = lax.reduce_precision(rest, exponent_bits=8, mantissa_bits=7)
    weight_low = rest - weight_mid
    table = jnp.concatenate(
        [rebin_offset.astype(jnp.float32), weight_high, weight_mid, weight_low], axis=1
    )
    halo = REACH + RIM
    lead_views = projected.shape[1]
    by_dest = projected.reshape(dev_count, row_count, lead_views, width)
    by_source = lax.all_to_all(by_dest, "dev", 0, 0, tiled=True)
    row_major = jnp.transpose(by_source, (1, 0, 2, 3)).reshape(
        row_count, dev_count * lead_views, width
    )

    def pack(data, params):
        flat = data.reshape(row_count * data.shape[1], width)
        params = params.reshape(-1)
        param_rows = -(-params.shape[0] // width)
        params = jnp.pad(params, (0, param_rows * width - params.shape[0]))
        params = params.astype(jnp.bfloat16).reshape(param_rows, width)
        return jnp.concatenate([flat, params], axis=0)

    def unpack(block, views_in, params_in):
        data = block[: row_count * views_in].reshape(row_count, views_in, width)
        params = block[row_count * views_in :].reshape(-1)[: params_in * 4 * block_count]
        return data, params.astype(jnp.float32).reshape(params_in, 4 * block_count)

    group_idx = lax.axis_index("group")
    if group_count == 2:
        first = group_idx == 0
        swap = [(0, 1), (1, 0)]
        plain = jnp.concatenate([rebin_offset.astype(jnp.float32), rebin_weight], axis=1)
        edge = jnp.where(first, plain[view_count - RIM :], plain[:RIM])
        other_params = lax.ppermute(edge, "group", swap)
        blank_params = jnp.zeros_like(other_params)
        params = jnp.where(
            first,
            jnp.concatenate([blank_params, plain, other_params], axis=0),
            jnp.concatenate([other_params, plain, blank_params], axis=0),
        )
        outgoing = jnp.where(first, row_major[:, view_count - halo :], row_major[:, :halo])
        other_data = lax.ppermute(outgoing, "group", swap)
        blank_data = jnp.zeros_like(other_data)
        extended = jnp.where(
            first,
            jnp.concatenate([blank_data, row_major, other_data], axis=1),
            jnp.concatenate([other_data, row_major, blank_data], axis=1),
        )
        bounds = jnp.stack([view_start, total_views]).astype(jnp.int32)
        return rebin_dual(extended, params, bounds, kern_first, kern_second, kern_last)
    else:
        head = pack(row_major[:, :halo], table[:RIM])
        tail = pack(row_major[:, view_count - halo :], table[view_count - RIM :])
        forward = [(i, i + 1) for i in range(group_count - 1)]
        backward = [(i + 1, i) for i in range(group_count - 1)]
        low_data, low_params = unpack(lax.ppermute(tail, "group", forward), halo, RIM)
        high_data, high_params = unpack(lax.ppermute(head, "group", backward), halo, RIM)
        extended = jnp.concatenate([low_data, row_major, high_data], axis=1)
        params = jnp.concatenate([low_params, table, high_params], axis=0)
    weights = params[:, block_count : 2 * block_count] + (
        params[:, 2 * block_count : 3 * block_count] + params[:, 3 * block_count :]
    )
    params = jnp.concatenate([params[:, :block_count], weights], axis=1)
    bounds = jnp.stack([view_start, total_views]).astype(jnp.int32)
    return rebin_dual(extended, params, bounds, kern_first, kern_second, kern_last)


def solution(mesh):
    return jax.shard_map(
        local,
        mesh=mesh,
        in_specs=(
            P(None, ("group", "dev"), None),
            P(None, ("group", "dev"), None),
            P(),
            P(),
            P(),
            P("group", None),
            P("group", None),
            P(),
            P(),
            P(),
        ),
        out_specs=P("dev", "group", None),
        check_vma=False,
    )
```

```python
import functools

import jax
import jax.numpy as jnp
from jax import lax
from jax.experimental import pallas as pl
from jax.experimental.pallas import tpu as pltpu
from jax.sharding import PartitionSpec as P

REACH = 8
RIM = 2


def conv_kernel(
    table_ref,
    bounds_ref,
    ext_ref,
    w1_ref,
    w2_ref,
    kl_ref,
    out_ref,
    sig_ref,
    feat_ref,
    dual_ref,
    *,
    sig_views,
    block_count,
    col_block,
    channels,
):
    width = block_count * col_block
    first_views = sig_views - 2
    out_views = sig_views - 4
    view_start = bounds_ref[0]
    total_views = bounds_ref[1]
    lane = lax.broadcasted_iota(jnp.int32, (1, width), 1)
    sig_ref[3 * sig_views :, :] = jnp.zeros((sig_ref.shape[0] - 3 * sig_views, width), jnp.float32)
    for u in range(sig_views):
        pos = view_start - RIM + u
        keep = ((pos >= 0) & (pos < total_views)).astype(jnp.float32)
        for k in range(block_count):
            entry = u * 2 * block_count + k
            low = u + table_ref[entry].astype(jnp.int32) + REACH
            frac = table_ref[entry + block_count]
            cols = pl.ds(k * col_block, col_block)
            lower = ext_ref[0, low, :, cols]
            upper = ext_ref[0, low + 1, :, cols]
            value = ((1.0 - frac) * lower + frac * upper).astype(jnp.bfloat16)
            sig_ref[3 * u + 1 : 3 * u + 2, cols] = value.astype(jnp.float32) * keep
        row = sig_ref[3 * u + 1 : 3 * u + 2, :]
        sig_ref[3 * u : 3 * u + 1, :] = jnp.where(lane >= 1, pltpu.roll(row, 1, 1), 0.0)
        sig_ref[3 * u + 2 : 3 * u + 3, :] = jnp.where(
            lane < width - 1, pltpu.roll(row, width - 1, 1), 0.0
        )
    col = lax.broadcasted_iota(jnp.int32, (channels, width), 1)
    keep_left = col >= 1
    keep_right = col < width - 1
    w1 = w1_ref[...]
    for u in range(first_views):
        taps = sig_ref[3 * u : 3 * u + 16, :].astype(jnp.bfloat16)
        pos = view_start - 1 + u
        scale = ((pos >= 0) & (pos < total_views)).astype(jnp.bfloat16)
        hidden = jnp.dot(w1 * scale, taps, preferred_element_type=jnp.float32)
        hidden = jnp.maximum(hidden, 0.0).astype(jnp.bfloat16)
        feat_ref[u * channels : (u + 1) * channels, :] = hidden
    w2 = w2_ref[...]
    kl = kl_ref[...]
    pair = 2 if out_views % 2 == 0 else 1
    for v0 in range(0, out_views, pair):
        window = jnp.concatenate(
            [feat_ref[v * channels : (v + 3) * channels, :] for v in range(v0, v0 + pair)],
            axis=1,
        )
        parts = jnp.dot(w2, window, preferred_element_type=jnp.float32)
        for j in range(pair):
            v = v0 + j
            part = parts[:, j * width : (j + 1) * width]
            second = part[channels : 2 * channels]
            second = second + jnp.where(keep_left, pltpu.roll(part[:channels], 1, 1), 0.0)
            second = second + jnp.where(
                keep_right, pltpu.roll(part[2 * channels :], width - 1, 1), 0.0
            )
            second = jnp.maximum(second, 0.0).astype(jnp.bfloat16).astype(jnp.float32)
            mix = jnp.sum(kl * second, axis=0, keepdims=True)
            centre = sig_ref[3 * (v + 2) + 1 : 3 * (v + 2) + 2, :]
            dual_ref[v : v + 1, :] = centre + mix
    out_ref[0] = dual_ref[...].astype(out_ref.dtype)


def rebin_dual(extended, table, bounds, kern_first, kern_second, kern_last):
    rows, ext_views, width = extended.shape
    sig_views = table.shape[0]
    block_count = table.shape[1] // 2
    col_block = width // block_count
    channels = kern_first.shape[0]
    first_views = sig_views - 2
    out_views = sig_views - 4
    pad_rows = -(-(3 * first_views + 13) // 8) * 8
    w1 = jnp.pad(kern_first.reshape(channels, 9), ((0, 0), (0, 7)))
    w2 = jnp.transpose(kern_second, (3, 0, 2, 1)).reshape(3 * channels, 3 * channels)
    kl = kern_last.astype(jnp.float32).reshape(channels, 1)
    kernel = functools.partial(
        conv_kernel,
        sig_views=sig_views,
        block_count=block_count,
        col_block=col_block,
        channels=channels,
    )
    grid_spec = pltpu.PrefetchScalarGridSpec(
        num_scalar_prefetch=2,
        grid=(rows,),
        in_specs=[
            pl.BlockSpec((1, ext_views, 1, width), lambda r, *_: (r, 0, 0, 0)),
            pl.BlockSpec((channels, 16), lambda r, *_: (0, 0)),
            pl.BlockSpec((3 * channels, 3 * channels), lambda r, *_: (0, 0)),
            pl.BlockSpec((channels, 1), lambda r, *_: (0, 0)),
        ],
        out_specs=pl.BlockSpec((1, out_views, width), lambda r, *_: (r, 0, 0)),
        scratch_shapes=[
            pltpu.VMEM((pad_rows, width), jnp.float32),
            pltpu.VMEM((first_views * channels, width), jnp.bfloat16),
            pltpu.VMEM((out_views, width), jnp.float32),
        ],
    )
    return pl.pallas_call(
        kernel,
        out_shape=jax.ShapeDtypeStruct((rows, out_views, width), jnp.bfloat16),
        grid_spec=grid_spec,
    )(
        table.reshape(-1),
        bounds,
        extended.astype(jnp.float32).reshape(rows, ext_views, 1, width),
        w1.astype(jnp.bfloat16),
        w2.astype(jnp.bfloat16),
        kl,
    )


def prepare(mantissa, exponent, poly_square, poly_cube):
    lead_rows, lead_views, width_all = mantissa.shape
    block_count = exponent.shape[2]
    counts = mantissa.astype(jnp.float32).reshape(
        lead_rows, lead_views, block_count, width_all // block_count
    )
    counts = counts * jnp.exp2(-exponent.astype(jnp.float32))[..., None]
    line_int = -jnp.log(counts).reshape(lead_rows, lead_views, width_all)
    hardened = (
        line_int + poly_square * line_int * line_int + poly_cube * line_int * line_int * line_int
    )
    return hardened.astype(jnp.bfloat16)


def resample(hardened, col_map):
    shape_in = hardened.shape
    flat = hardened.reshape(-1, shape_in[2])
    product = jnp.dot(flat, col_map, preferred_element_type=jnp.float32)
    return product.astype(jnp.bfloat16).reshape(shape_in)


def local(
    mantissa,
    exponent,
    poly_square,
    poly_cube,
    col_map,
    rebin_offset,
    rebin_weight,
    kern_first,
    kern_second,
    kern_last,
):
    projected = resample(prepare(mantissa, exponent, poly_square, poly_cube), col_map)
    lead_rows, _, width = projected.shape
    group_count = lax.axis_size("group")
    dev_count = lax.axis_size("dev")
    row_count = lead_rows // dev_count
    block_count = rebin_offset.shape[1]
    view_count = rebin_offset.shape[0]
    total_views = view_count * group_count
    view_start = lax.axis_index("group") * view_count

    weight_high = lax.reduce_precision(rebin_weight, exponent_bits=8, mantissa_bits=7)
    rest = rebin_weight - weight_high
    weight_mid = lax.reduce_precision(rest, exponent_bits=8, mantissa_bits=7)
    weight_low = rest - weight_mid
    table = jnp.concatenate(
        [rebin_offset.astype(jnp.float32), weight_high, weight_mid, weight_low], axis=1
    )
    halo = REACH + RIM
    lead_views = projected.shape[1]
    by_dest = projected.reshape(dev_count, row_count, lead_views, width)
    by_source = lax.all_to_all(by_dest, "dev", 0, 0, tiled=True)
    row_major = jnp.transpose(by_source, (1, 0, 2, 3)).reshape(
        row_count, dev_count * lead_views, width
    )

    def pack(data, params):
        flat = data.reshape(row_count * data.shape[1], width)
        params = params.reshape(-1)
        param_rows = -(-params.shape[0] // width)
        params = jnp.pad(params, (0, param_rows * width - params.shape[0]))
        params = params.astype(jnp.bfloat16).reshape(param_rows, width)
        return jnp.concatenate([flat, params], axis=0)

    def unpack(block, views_in, params_in):
        data = block[: row_count * views_in].reshape(row_count, views_in, width)
        params = block[row_count * views_in :].reshape(-1)[: params_in * 4 * block_count]
        return data, params.astype(jnp.float32).reshape(params_in, 4 * block_count)

    group_idx = lax.axis_index("group")
    if group_count == 2:
        first = group_idx == 0
        swap = [(0, 1), (1, 0)]
        plain = jnp.concatenate([rebin_offset.astype(jnp.float32), rebin_weight], axis=1)
        edge = jnp.where(first, plain[view_count - RIM :], plain[:RIM])
        other_params = lax.ppermute(edge, "group", swap)
        blank_params = jnp.zeros_like(other_params)
        params = jnp.where(
            first,
            jnp.concatenate([blank_params, plain, other_params], axis=0),
            jnp.concatenate([other_params, plain, blank_params], axis=0),
        )
        outgoing = jnp.where(first, row_major[:, view_count - halo :], row_major[:, :halo])
        other_data = lax.ppermute(outgoing, "group", swap)
        blank_data = jnp.zeros_like(other_data)
        extended = jnp.where(
            first,
            jnp.concatenate([blank_data, row_major, other_data], axis=1),
            jnp.concatenate([other_data, row_major, blank_data], axis=1),
        )
        bounds = jnp.stack([view_start, total_views]).astype(jnp.int32)
        return rebin_dual(extended, params, bounds, kern_first, kern_second, kern_last)
    else:
        head = pack(row_major[:, :halo], table[:RIM])
        tail = pack(row_major[:, view_count - halo :], table[view_count - RIM :])
        forward = [(i, i + 1) for i in range(group_count - 1)]
        backward = [(i + 1, i) for i in range(group_count - 1)]
        low_data, low_params = unpack(lax.ppermute(tail, "group", forward), halo, RIM)
        high_data, high_params = unpack(lax.ppermute(head, "group", backward), halo, RIM)
        extended = jnp.concatenate([low_data, row_major, high_data], axis=1)
        params = jnp.concatenate([low_params, table, high_params], axis=0)
    weights = params[:, block_count : 2 * block_count] + (
        params[:, 2 * block_count : 3 * block_count] + params[:, 3 * block_count :]
    )
    params = jnp.concatenate([params[:, :block_count], weights], axis=1)
    bounds = jnp.stack([view_start, total_views]).astype(jnp.int32)
    return rebin_dual(extended, params, bounds, kern_first, kern_second, kern_last)


def solution(mesh):
    return jax.shard_map(
        local,
        mesh=mesh,
        in_specs=(
            P(None, ("group", "dev"), None),
            P(None, ("group", "dev"), None),
            P(),
            P(),
            P(),
            P("group", None),
            P("group", None),
            P(),
            P(),
            P(),
        ),
        out_specs=P("dev", "group", None),
        check_vma=False,
    )
```

```python
import functools

import jax
import jax.numpy as jnp
from jax import lax
from jax.experimental import pallas as pl
from jax.experimental.pallas import tpu as pltpu
from jax.sharding import PartitionSpec as P

REACH = 8
RIM = 2


def conv_kernel(
    table_ref,
    bounds_ref,
    ext_ref,
    w1_ref,
    w2_ref,
    kl_ref,
    out_ref,
    sig_ref,
    feat_ref,
    dual_ref,
    *,
    sig_views,
    block_count,
    col_block,
    channels,
):
    width = block_count * col_block
    first_views = sig_views - 2
    out_views = sig_views - 4
    view_start = bounds_ref[0]
    total_views = bounds_ref[1]
    lane = lax.broadcasted_iota(jnp.int32, (1, width), 1)
    sig_ref[3 * sig_views :, :] = jnp.zeros((sig_ref.shape[0] - 3 * sig_views, width), jnp.float32)
    for u in range(sig_views):
        pos = view_start - RIM + u
        keep = ((pos >= 0) & (pos < total_views)).astype(jnp.float32)
        for k in range(block_count):
            entry = u * 2 * block_count + k
            low = u + table_ref[entry].astype(jnp.int32) + REACH
            frac = table_ref[entry + block_count]
            cols = pl.ds(k * col_block, col_block)
            lower = ext_ref[0, low, :, cols].astype(jnp.float32)
            upper = ext_ref[0, low + 1, :, cols].astype(jnp.float32)
            value = ((1.0 - frac) * lower + frac * upper).astype(jnp.bfloat16)
            sig_ref[3 * u + 1 : 3 * u + 2, cols] = value.astype(jnp.float32) * keep
        row = sig_ref[3 * u + 1 : 3 * u + 2, :]
        sig_ref[3 * u : 3 * u + 1, :] = jnp.where(lane >= 1, pltpu.roll(row, 1, 1), 0.0)
        sig_ref[3 * u + 2 : 3 * u + 3, :] = jnp.where(
            lane < width - 1, pltpu.roll(row, width - 1, 1), 0.0
        )
    col = lax.broadcasted_iota(jnp.int32, (channels, width), 1)
    keep_left = col >= 1
    keep_right = col < width - 1
    w1 = w1_ref[...]
    for u in range(first_views):
        taps = sig_ref[3 * u : 3 * u + 16, :].astype(jnp.bfloat16)
        pos = view_start - 1 + u
        scale = ((pos >= 0) & (pos < total_views)).astype(jnp.bfloat16)
        hidden = jnp.dot(w1 * scale, taps, preferred_element_type=jnp.float32)
        hidden = jnp.maximum(hidden, 0.0).astype(jnp.bfloat16)
        feat_ref[u * channels : (u + 1) * channels, :] = hidden
    w2 = w2_ref[...]
    kl = kl_ref[...]
    for v in range(out_views):
        window = feat_ref[v * channels : (v + 3) * channels, :]
        part = jnp.dot(w2, window, preferred_element_type=jnp.float32)
        second = part[channels : 2 * channels]
        second = second + jnp.where(keep_left, pltpu.roll(part[:channels], 1, 1), 0.0)
        second = second + jnp.where(
            keep_right, pltpu.roll(part[2 * channels :], width - 1, 1), 0.0
        )
        second = jnp.maximum(second, 0.0).astype(jnp.bfloat16).astype(jnp.float32)
        mix = jnp.sum(kl * second, axis=0, keepdims=True)
        centre = sig_ref[3 * (v + 2) + 1 : 3 * (v + 2) + 2, :]
        dual_ref[v : v + 1, :] = centre + mix
    out_ref[0] = dual_ref[...].astype(out_ref.dtype)


def rebin_dual(extended, table, bounds, kern_first, kern_second, kern_last):
    rows, ext_views, width = extended.shape
    sig_views = table.shape[0]
    block_count = table.shape[1] // 2
    col_block = width // block_count
    channels = kern_first.shape[0]
    first_views = sig_views - 2
    out_views = sig_views - 4
    pad_rows = -(-(3 * first_views + 13) // 8) * 8
    w1 = jnp.pad(kern_first.reshape(channels, 9), ((0, 0), (0, 7)))
    w2 = jnp.transpose(kern_second, (3, 0, 2, 1)).reshape(3 * channels, 3 * channels)
    kl = kern_last.astype(jnp.float32).reshape(channels, 1)
    kernel = functools.partial(
        conv_kernel,
        sig_views=sig_views,
        block_count=block_count,
        col_block=col_block,
        channels=channels,
    )
    grid_spec = pltpu.PrefetchScalarGridSpec(
        num_scalar_prefetch=2,
        grid=(rows,),
        in_specs=[
            pl.BlockSpec((1, ext_views, 1, width), lambda r, *_: (r, 0, 0, 0)),
            pl.BlockSpec((channels, 16), lambda r, *_: (0, 0)),
            pl.BlockSpec((3 * channels, 3 * channels), lambda r, *_: (0, 0)),
            pl.BlockSpec((channels, 1), lambda r, *_: (0, 0)),
        ],
        out_specs=pl.BlockSpec((1, out_views, width), lambda r, *_: (r, 0, 0)),
        scratch_shapes=[
            pltpu.VMEM((pad_rows, width), jnp.float32),
            pltpu.VMEM((first_views * channels, width), jnp.bfloat16),
            pltpu.VMEM((out_views, width), jnp.float32),
        ],
    )
    return pl.pallas_call(
        kernel,
        out_shape=jax.ShapeDtypeStruct((rows, out_views, width), jnp.bfloat16),
        grid_spec=grid_spec,
    )(
        table.reshape(-1),
        bounds,
        extended.reshape(rows, ext_views, 1, width),
        w1.astype(jnp.bfloat16),
        w2.astype(jnp.bfloat16),
        kl,
    )


def prepare(mantissa, exponent, poly_square, poly_cube):
    lead_rows, lead_views, width_all = mantissa.shape
    block_count = exponent.shape[2]
    counts = mantissa.astype(jnp.float32).reshape(
        lead_rows, lead_views, block_count, width_all // block_count
    )
    counts = counts * jnp.exp2(-exponent.astype(jnp.float32))[..., None]
    line_int = -jnp.log(counts).reshape(lead_rows, lead_views, width_all)
    hardened = (
        line_int + poly_square * line_int * line_int + poly_cube * line_int * line_int * line_int
    )
    return hardened.astype(jnp.bfloat16)


def resample(hardened, col_map):
    shape_in = hardened.shape
    flat = hardened.reshape(-1, shape_in[2])
    product = jnp.dot(flat, col_map, preferred_element_type=jnp.float32)
    return product.astype(jnp.bfloat16).reshape(shape_in)


def local(
    mantissa,
    exponent,
    poly_square,
    poly_cube,
    col_map,
    rebin_offset,
    rebin_weight,
    kern_first,
    kern_second,
    kern_last,
):
    projected = resample(prepare(mantissa, exponent, poly_square, poly_cube), col_map)
    lead_rows, _, width = projected.shape
    group_count = lax.axis_size("group")
    dev_count = lax.axis_size("dev")
    row_count = lead_rows // dev_count
    block_count = rebin_offset.shape[1]
    view_count = rebin_offset.shape[0]
    total_views = view_count * group_count
    view_start = lax.axis_index("group") * view_count

    weight_high = lax.reduce_precision(rebin_weight, exponent_bits=8, mantissa_bits=7)
    rest = rebin_weight - weight_high
    weight_mid = lax.reduce_precision(rest, exponent_bits=8, mantissa_bits=7)
    weight_low = rest - weight_mid
    table = jnp.concatenate(
        [rebin_offset.astype(jnp.float32), weight_high, weight_mid, weight_low], axis=1
    )
    halo = REACH + RIM
    lead_views = projected.shape[1]
    by_dest = projected.reshape(dev_count, row_count, lead_views, width)
    by_source = lax.all_to_all(by_dest, "dev", 0, 0, tiled=True)
    row_major = jnp.transpose(by_source, (1, 0, 2, 3)).reshape(
        row_count, dev_count * lead_views, width
    )

    def pack(data, params):
        flat = data.reshape(row_count * data.shape[1], width)
        params = params.reshape(-1)
        param_rows = -(-params.shape[0] // width)
        params = jnp.pad(params, (0, param_rows * width - params.shape[0]))
        params = params.astype(jnp.bfloat16).reshape(param_rows, width)
        return jnp.concatenate([flat, params], axis=0)

    def unpack(block, views_in, params_in):
        data = block[: row_count * views_in].reshape(row_count, views_in, width)
        params = block[row_count * views_in :].reshape(-1)[: params_in * 4 * block_count]
        return data, params.astype(jnp.float32).reshape(params_in, 4 * block_count)

    group_idx = lax.axis_index("group")
    if group_count == 2:
        first = group_idx == 0
        swap = [(0, 1), (1, 0)]
        plain = jnp.concatenate([rebin_offset.astype(jnp.float32), rebin_weight], axis=1)
        edge = jnp.where(first, plain[view_count - RIM :], plain[:RIM])
        other_params = lax.ppermute(edge, "group", swap)
        blank_params = jnp.zeros_like(other_params)
        params = jnp.where(
            first,
            jnp.concatenate([blank_params, plain, other_params], axis=0),
            jnp.concatenate([other_params, plain, blank_params], axis=0),
        )
        outgoing = jnp.where(first, row_major[:, view_count - halo :], row_major[:, :halo])
        other_data = lax.ppermute(outgoing, "group", swap)
        blank_data = jnp.zeros_like(other_data)
        extended = jnp.where(
            first,
            jnp.concatenate([blank_data, row_major, other_data], axis=1),
            jnp.concatenate([other_data, row_major, blank_data], axis=1),
        )
        bounds = jnp.stack([view_start, total_views]).astype(jnp.int32)
        return rebin_dual(extended, params, bounds, kern_first, kern_second, kern_last)
    else:
        head = pack(row_major[:, :halo], table[:RIM])
        tail = pack(row_major[:, view_count - halo :], table[view_count - RIM :])
        forward = [(i, i + 1) for i in range(group_count - 1)]
        backward = [(i + 1, i) for i in range(group_count - 1)]
        low_data, low_params = unpack(lax.ppermute(tail, "group", forward), halo, RIM)
        high_data, high_params = unpack(lax.ppermute(head, "group", backward), halo, RIM)
        extended = jnp.concatenate([low_data, row_major, high_data], axis=1)
        params = jnp.concatenate([low_params, table, high_params], axis=0)
    weights = params[:, block_count : 2 * block_count] + (
        params[:, 2 * block_count : 3 * block_count] + params[:, 3 * block_count :]
    )
    params = jnp.concatenate([params[:, :block_count], weights], axis=1)
    bounds = jnp.stack([view_start, total_views]).astype(jnp.int32)
    return rebin_dual(extended, params, bounds, kern_first, kern_second, kern_last)


def solution(mesh):
    return jax.shard_map(
        local,
        mesh=mesh,
        in_specs=(
            P(None, ("group", "dev"), None),
            P(None, ("group", "dev"), None),
            P(),
            P(),
            P(),
            P("group", None),
            P("group", None),
            P(),
            P(),
            P(),
        ),
        out_specs=P("dev", "group", None),
        check_vma=False,
    )
```
